256 devices in a mesh: seq: 32 (over z_hi, x, core), ch: 8 (over z_lo, y).
Axes of the slice: x: 4, y: 4, z: 8 (z_hi: 4, z_lo: 2; z = z_hi * 2 + z_lo), core: 2. Of those that a mesh axis runs over, the one named last changes fastest.
Arguments:
- query_in: bfloat16 [16384, 2048], P('seq', 'ch'), may hold values from -6 to 6
- key_in: bfloat16 [16384, 2048], P('seq', 'ch'), may hold values from -6 to 6
- value_in: bfloat16 [16384, 2048], P('seq', 'ch'), may hold values from -6 to 6
- filter_taps: float32 [16384, 2048], P('seq', 'ch'), may hold values from -1 to 1
- skip_gain: float32 [2048], P('ch'), may hold values from 0.5 to 1.5
- out_weight: bfloat16 [2048, 2048], P('ch'), may hold values from -0.125 to 0.125
- out_grad: bfloat16 [16384, 2048], P('seq', 'ch'), may hold values from -6 to 6
Outputs:
- mixed_out: bfloat16 [16384, 2048], P('seq', 'ch')
- query_grad: bfloat16 [16384, 2048], P('seq', 'ch')
- key_grad: bfloat16 [16384, 2048], P('seq', 'ch')
- value_grad: bfloat16 [16384, 2048], P('seq', 'ch')
The draws below stay inside these ranges and needn't reach their ends.
All inputs are finite; a program needn't handle non-finite values.
Results may differ from the reference program's by a relative error of at most 0.0049.
Values may be sent and summed in bfloat16 or wider, within the bound.
A program may use at most 64 MiB of HBM per device.

```python
import math
import jax
import jax.numpy as jnp
from jax import lax

D = 2048
TOKENS = 16384


def draw_filter_taps(key, part):
    key_rate, key_amp = jax.random.split(key, 2)
    positions = jnp.arange(TOKENS, dtype=jnp.float32)[:, None]
    fast_log = math.log(1.0 / 32.0)
    slow_log = math.log(1.0 / TOKENS)
    decay_rates = jnp.exp(jax.random.uniform(key_rate, (D,), dtype=jnp.float32, minval=slow_log, maxval=fast_log))
    amplitude = jnp.clip(jax.random.normal(key_amp, (TOKENS, D), dtype=jnp.float32), -4.0, 4.0)
    norm_scale = jnp.sqrt(2.0 * decay_rates / (1.0 - jnp.exp(-2.0 * decay_rates * TOKENS)))
    return jnp.clip(amplitude * jnp.exp(-decay_rates * positions) * norm_scale, -1.0, 1.0)


def level_of(key, extent, cuts, low, largest):
    def one(axis_at, shards_of):
        heights = jax.random.uniform(jax.random.fold_in(jax.random.fold_in(key, 6), axis_at), (shards_of,), jnp.float32, low / len(cuts), largest / len(cuts))
        return jnp.repeat(jnp.exp(heights), extent[axis_at] // shards_of).reshape((-1,) + (1,) * (len(extent) - axis_at - 1))

    gain = one(*cuts[0])
    for cut in cuts[1:]:
        gain = gain * one(*cut)
    return gain


def bell_draw(own_key, extent, width, most, shards=(), kind=jnp.bfloat16):
    entries = jax.random.normal(own_key, extent, jnp.float32) * width
    if len(shards) > 0:
        entries = level_of(own_key, extent, shards, -0.22, 0.18) * entries
    return jnp.clip(entries, min=-most, max=most).astype(kind)


def setup_inputs(seed: int = 0) -> dict:
    seeds = jax.random.split(jax.random.key(seed), 8)
    return {
        "query_in": bell_draw(seeds[0], (TOKENS, D), 1.0, 6.0, ((0, 32), (1, 8))),
        "key_in": bell_draw(seeds[1], (TOKENS, D), 1.0, 6.0, ((0, 32), (1, 8))),
        "value_in": bell_draw(seeds[2], (TOKENS, D), 1.0, 6.0, ((0, 32), (1, 8))),
        "filter_taps": draw_filter_taps(jax.random.fold_in(seeds[7], 71), 0),
        "skip_gain": jnp.clip(0.5 + 1.0 * jax.random.uniform(seeds[4], (D,), jnp.float32) ** level_of(seeds[4], (D,), ((0, 8),), -0.2, 0.2), 0.5, 1.5),
        "out_weight": bell_draw(seeds[5], (D, D), D ** -0.5, 0.125, ((0, 8),)),
        "out_grad": bell_draw(seeds[6], (TOKENS, D), 1.0, 6.0, ((0, 32), (1, 8))),
    }


def plain_product(taps_spec, signal_spec):
    return taps_spec * signal_spec


def adjoint_product(taps_spec, signal_spec):
    return jnp.conj(taps_spec) * signal_spec


def filter_blocks(signal, taps, combine):
    length, channels = signal.shape
    block_size = math.gcd(channels, 128)
    block_count = channels // block_size
    signal_blocks = signal.reshape(length, block_count, block_size).transpose(1, 0, 2)
    taps_blocks = taps.reshape(length, block_count, block_size).transpose(1, 0, 2)

    def apply_block(operands):
        signal_block, taps_block = operands
        signal_spec = jnp.fft.rfft(signal_block, n=2 * length, axis=0)
        taps_spec = jnp.fft.rfft(taps_block, n=2 * length, axis=0)
        return jnp.fft.irfft(combine(taps_spec, signal_spec), n=2 * length, axis=0)[:length]

    result = lax.map(apply_block, (signal_blocks, taps_blocks))
    return result.transpose(1, 0, 2).reshape(length, channels)


def reference(query_in, key_in, value_in, filter_taps, skip_gain, out_weight, out_grad):
    query_wide = query_in.astype(jnp.float32)
    mixed_in = key_in.astype(jnp.float32) * value_in.astype(jnp.float32)
    conv_out = filter_blocks(mixed_in, filter_taps, plain_product) + skip_gain * mixed_in
    gated_out = (query_wide * conv_out).astype(jnp.bfloat16)
    mixed_out = jnp.dot(gated_out, out_weight, preferred_element_type=jnp.float32).astype(jnp.bfloat16)
    grad_gated = jnp.dot(out_grad, out_weight.T, preferred_element_type=jnp.float32)
    query_grad = (grad_gated * conv_out).astype(jnp.bfloat16)
    grad_conv = grad_gated * query_wide
    grad_mixed = filter_blocks(grad_conv, filter_taps, adjoint_product) + skip_gain * grad_conv
    key_grad = (grad_mixed * value_in.astype(jnp.float32)).astype(jnp.bfloat16)
    value_grad = (grad_mixed * key_in.astype(jnp.float32)).astype(jnp.bfloat16)
    return mixed_out, query_grad, key_grad, value_grad
```

```python
import functools
import math

import jax
import jax.numpy as jnp
import numpy as np
from jax import lax
from jax.experimental import pallas as pl
from jax.experimental.pallas import tpu as pltpu
from jax.sharding import PartitionSpec as P

F32 = jnp.float32
BF16 = jnp.bfloat16
MESH = pl.DeviceIdType.MESH

R = 128
L = R * R


def split_table(table):
    high = table.astype(np.float32).astype(jnp.bfloat16)
    low = (table - high.astype(np.float64)).astype(np.float32).astype(jnp.bfloat16)
    return high, low


def tables():
    n = np.arange(R, dtype=np.float64)
    p = n + 0.25
    first = np.exp(-2j * math.pi * np.outer(p, n) / R)
    turn = np.exp(-2j * math.pi * np.outer(p, n) / L)
    second = np.exp(-2j * math.pi * np.outer(n, n) / R)
    forward_a = np.concatenate([first.real, first.imag], axis=0)
    forward_b = np.block([[second.real, second.imag], [-second.imag, second.real]])
    inverse_b = forward_b.T
    inverse_a = np.concatenate([first.real.T, first.imag.T], axis=1) / L
    fa_high, fa_low = split_table(forward_a)
    fb_high, fb_low = split_table(forward_b)
    ib_high, ib_low = split_table(inverse_b)
    ia_high, ia_low = split_table(inverse_a)
    return (
        np.concatenate([fa_high, fa_low], axis=0),
        fb_high,
        fb_low,
        ib_high,
        ib_low,
        ia_high,
        ia_low,
        turn.real.astype(np.float32),
        turn.imag.astype(np.float32),
    )


def split(values):
    high = values.astype(BF16)
    low = (values - high.astype(F32)).astype(BF16)
    return high, low


def dot(left, right):
    return jnp.dot(left, right, preferred_element_type=F32)


def layer_kernel(
    seq_count,
    ch_count,
    query,
    key,
    value,
    taps,
    skip,
    weight,
    out_grad,
    fa,
    fb_high,
    fb_low,
    ib_high,
    ib_low,
    ia_high,
    ia_low,
    turn_re,
    turn_im,
    mixed_out,
    query_grad,
    key_grad,
    value_grad,
    seq_send,
    seq_recv,
    stage,
    taps_spec,
    cotangents,
    gated_all,
    weight_cols,
    grad_gated,
    grad_conv,
    seq_send_sem,
    seq_recv_sem,
    ch_send_sem,
    ch_recv_sem,
):
    seq_me = lax.axis_index("seq")
    ch_me = lax.axis_index("ch")
    row_count = query.shape[0]
    blocks = row_count // R
    columns = query.shape[1]
    half = ch_count // 2
    pair = lax.rem(ch_me + half, ch_count)
    group = (ch_me // half) * half
    spot = lax.rem(ch_me, half)

    barrier = pltpu.get_barrier_semaphore()

    def greet_seq(step, carry):
        peer = lax.rem(seq_me + step, seq_count)
        pl.semaphore_signal(barrier, inc=1, device_id={"seq": peer}, device_id_type=MESH)
        return carry

    def greet_ch(step, carry):
        peer = lax.rem(ch_me + step, ch_count)
        pl.semaphore_signal(barrier, inc=1, device_id={"ch": peer}, device_id_type=MESH)
        return carry

    lax.fori_loop(1, seq_count, greet_seq, 0)
    lax.fori_loop(1, ch_count, greet_ch, 0)

    def rows(block):
        return slice(block * R, (block + 1) * R)

    def lay_out(which, block, values):
        turned = jnp.transpose(values).astype(BF16)
        seq_send[which, :, block] = turned.reshape(seq_count, columns // seq_count, R)

    def exchange(which):
        def step(index, carry):
            peer = lax.rem(seq_me + index, seq_count)
            pltpu.make_async_remote_copy(
                src_ref=seq_send.at[which, peer],
                dst_ref=seq_recv.at[which, seq_me],
                send_sem=seq_send_sem.at[which],
                recv_sem=seq_recv_sem.at[which],
                device_id={"seq": peer},
                device_id_type=MESH,
            ).start()
            return carry

        lax.fori_loop(1, seq_count, step, 0)
        seq_recv[which, seq_me] = seq_send[which, seq_me]

    def exchanged(which):
        return pltpu.make_async_remote_copy(
            src_ref=seq_send.at[which, pl.ds(0, seq_count - 1)],
            dst_ref=seq_recv.at[which, pl.ds(0, seq_count - 1)],
            send_sem=seq_send_sem.at[which],
            recv_sem=seq_recv_sem.at[which],
            device_id={"seq": lax.rem(seq_me + 1, seq_count)},
            device_id_type=MESH,
        )

    def share(source, target, slot, which):
        for step in range(1, half):
            peer = group + lax.rem(spot + step, half)
            pltpu.make_async_remote_copy(
                src_ref=source,
                dst_ref=target.at[slot],
                send_sem=ch_send_sem.at[which],
                recv_sem=ch_recv_sem.at[which],
                device_id={"ch": peer},
                device_id_type=MESH,
            ).start()

    def shared(target, which):
        return pltpu.make_async_remote_copy(
            src_ref=target.at[pl.ds(0, half - 1)],
            dst_ref=target.at[pl.ds(0, half - 1)],
            send_sem=ch_send_sem.at[which],
            recv_sem=ch_recv_sem.at[which],
            device_id={"ch": pair},
            device_id_type=MESH,
        )

    def across(source, target, slot, which):
        return pltpu.make_async_remote_copy(
            src_ref=source,
            dst_ref=target.at[slot],
            send_sem=ch_send_sem.at[which],
            recv_sem=ch_recv_sem.at[which],
            device_id={"ch": pair},
            device_id_type=MESH,
        )

    def to_stage(which):
        stage[...] = seq_recv[which].astype(F32).reshape(L // R * 8, R)

    def from_stage(which):
        seq_send[which] = stage[...].astype(BF16).reshape(seq_count, blocks, 8, R)

    def spectrum(channel):
        signal = stage[pl.ds(channel, R, stride=8), :].astype(BF16)
        both = dot(fa[...], signal)
        both = both[: 2 * R] + both[2 * R :]
        real, imag = both[:R], both[R:]
        turned_re = real * turn_re[...] - imag * turn_im[...]
        turned_im = real * turn_im[...] + imag * turn_re[...]
        high, low = split(jnp.concatenate([turned_re, turned_im], axis=1))
        out = dot(high, fb_high[...]) + dot(low, fb_high[...]) + dot(high, fb_low[...])
        return out[:, :R], out[:, R:]

    def signal_of(real, imag, channel):
        high, low = split(jnp.concatenate([real, imag], axis=1))
        back = dot(high, ib_high[...]) + dot(low, ib_high[...]) + dot(high, ib_low[...])
        real, imag = back[:, :R], back[:, R:]
        turned_re = real * turn_re[...] + imag * turn_im[...]
        turned_im = imag * turn_re[...] - real * turn_im[...]
        high, low = split(jnp.concatenate([turned_re, turned_im], axis=0))
        out = dot(ia_high[...], high) + dot(ia_high[...], low) + dot(ia_low[...], high)
        stage[pl.ds(channel, R, stride=8), :] = out

    def received(which, block):
        return jnp.transpose(seq_recv[which, :, block].astype(F32).reshape(columns, R))

    TAPS, MIXED, CONV, GRAD, BACK = range(5)
    COT_PAIR, COT_OWN, COT_FAR, GATED_PAIR, GATED_OWN, GATED_FAR, WEIGHT = range(7)

    for block in range(blocks):
        lay_out(TAPS, block, taps[rows(block), :])
    for block in range(blocks):
        lay_out(
            MIXED, block, key[rows(block), :].astype(F32) * value[rows(block), :].astype(F32)
        )

    pl.semaphore_wait(barrier, seq_count + ch_count - 2)

    across(out_grad, cotangents, ch_me, COT_PAIR).start()
    share(out_grad, cotangents, ch_me, COT_OWN)
    exchange(TAPS)
    exchange(MIXED)
    cotangents[ch_me] = out_grad[...]

    across(out_grad, cotangents, pair, COT_PAIR).wait_recv()
    share(cotangents.at[pair], cotangents, pair, COT_FAR)

    def send_weight(step, carry):
        peer = lax.rem(ch_me + step, ch_count)
        pltpu.make_async_remote_copy(
            src_ref=weight.at[:, pl.ds(pl.multiple_of(peer * columns, columns), columns)],
            dst_ref=weight_cols.at[ch_me],
            send_sem=ch_send_sem.at[WEIGHT],
            recv_sem=ch_recv_sem.at[WEIGHT],
            device_id={"ch": peer},
            device_id_type=MESH,
        ).start()
        return carry

    lax.fori_loop(1, ch_count, send_weight, 0)
    weight_cols[ch_me] = weight[:, pl.ds(pl.multiple_of(ch_me * columns, columns), columns)]

    exchanged(TAPS).wait_recv()
    to_stage(TAPS)

    def taps_step(channel, carry):
        real, imag = spectrum(channel)
        taps_spec[channel, :, :R] = real
        taps_spec[channel, :, R:] = imag
        return carry

    lax.fori_loop(0, 8, taps_step, 0)

    exchanged(MIXED).wait_recv()
    to_stage(MIXED)

    def mixed_step(channel, carry):
        real, imag = spectrum(channel)
        taps_re, taps_im = taps_spec[channel, :, :R], taps_spec[channel, :, R:]
        signal_of(real * taps_re - imag * taps_im, real * taps_im + imag * taps_re, channel)
        return carry

    lax.fori_loop(0, 8, mixed_step, 0)
    from_stage(CONV)
    exchange(CONV)

    shared(cotangents, COT_OWN).wait_recv()
    shared(cotangents, COT_FAR).wait_recv()
    for block in range(blocks):
        total = None
        for source in range(ch_count):
            term = lax.dot_general(
                cotangents[source, rows(block), :],
                weight[:, source * columns : (source + 1) * columns],
                (((1,), (1,)), ((), ())),
                preferred_element_type=F32,
            )
            total = term if total is None else total + term
        grad_gated[rows(block), :] = total
        product = total * query[rows(block), :].astype(F32)
        grad_conv[rows(block), :] = product
        lay_out(GRAD, block, product)
    exchange(GRAD)

    exchanged(CONV).wait_recv()
    gains = skip[...]
    for block in range(blocks):
        mixed = key[rows(block), :].astype(F32) * value[rows(block), :].astype(F32)
        conv = received(CONV, block) + gains * mixed
        gated_all[ch_me, rows(block), :] = (query[rows(block), :].astype(F32) * conv).astype(BF16)
        query_grad[rows(block), :] = (grad_gated[rows(block), :] * conv).astype(BF16)
    across(gated_all.at[ch_me], gated_all, ch_me, GATED_PAIR).start()
    share(gated_all.at[ch_me], gated_all, ch_me, GATED_OWN)

    exchanged(GRAD).wait_recv()
    to_stage(GRAD)

    def grad_step(channel, carry):
        real, imag = spectrum(channel)
        taps_re, taps_im = taps_spec[channel, :, :R], taps_spec[channel, :, R:]
        signal_of(taps_re * real + taps_im * imag, taps_re * imag - taps_im * real, channel)
        return carry

    lax.fori_loop(0, 8, grad_step, 0)
    from_stage(BACK)
    exchange(BACK)

    across(gated_all.at[ch_me], gated_all, pair, GATED_PAIR).wait_recv()
    share(gated_all.at[pair], gated_all, pair, GATED_FAR)

    exchanged(BACK).wait_recv()
    for block in range(blocks):
        total = received(BACK, block) + gains * grad_conv[rows(block), :]
        key_grad[rows(block), :] = (total * value[rows(block), :].astype(F32)).astype(BF16)
        value_grad[rows(block), :] = (total * key[rows(block), :].astype(F32)).astype(BF16)

    pltpu.make_async_remote_copy(
        src_ref=weight_cols.at[pl.ds(0, ch_count - 1)],
        dst_ref=weight_cols.at[pl.ds(0, ch_count - 1)],
        send_sem=ch_send_sem.at[WEIGHT],
        recv_sem=ch_recv_sem.at[WEIGHT],
        device_id={"ch": pair},
        device_id_type=MESH,
    ).wait()
    shared(gated_all, GATED_OWN).wait_recv()
    shared(gated_all, GATED_FAR).wait_recv()
    for block in range(blocks):
        total = None
        for source in range(ch_count):
            term = dot(gated_all[source, rows(block), :], weight_cols[source])
            total = term if total is None else total + term
        mixed_out[rows(block), :] = total.astype(BF16)

    for which in range(5):
        exchanged(which).wait_send()
    across(out_grad, cotangents, ch_me, COT_PAIR).wait_send()
    across(gated_all.at[ch_me], gated_all, ch_me, GATED_PAIR).wait_send()
    for which in (COT_OWN, COT_FAR):
        shared(cotangents, which).wait_send()
    for which in (GATED_OWN, GATED_FAR):
        shared(gated_all, which).wait_send()


def on_device(query_in, key_in, value_in, filter_taps, skip_gain, out_weight, out_grad):
    seq_count = lax.axis_size("seq")
    ch_count = lax.axis_size("ch")
    row_count, columns = query_in.shape
    blocks = row_count // R
    operands = (
        query_in,
        key_in,
        value_in,
        filter_taps,
        skip_gain.reshape(1, columns),
        out_weight,
        out_grad,
    ) + tuple(jnp.asarray(table) for table in tables())
    in_vmem = pl.BlockSpec(memory_space=pltpu.VMEM)
    return pl.pallas_call(
        functools.partial(layer_kernel, seq_count, ch_count),
        out_shape=[jax.ShapeDtypeStruct((row_count, columns), BF16)] * 4,
        in_specs=[in_vmem] * len(operands),
        out_specs=[in_vmem] * 4,
        scratch_shapes=[
            pltpu.VMEM((5, seq_count, blocks, 8, R), BF16),
            pltpu.VMEM((5, seq_count, blocks, 8, R), BF16),
            pltpu.VMEM((L // R * 8, R), F32),
            pltpu.VMEM((8, R, 2 * R), F32),
            pltpu.VMEM((ch_count, row_count, columns), BF16),
            pltpu.VMEM((ch_count, row_count, columns), BF16),
            pltpu.VMEM((ch_count, columns, columns), BF16),
            pltpu.VMEM((row_count, columns), F32),
            pltpu.VMEM((row_count, columns), F32),
            pltpu.SemaphoreType.DMA((5,)),
            pltpu.SemaphoreType.DMA((5,)),
            pltpu.SemaphoreType.DMA((7,)),
            pltpu.SemaphoreType.DMA((7,)),
        ],
        compiler_params=pltpu.CompilerParams(
            collective_id=0, has_side_effects=True, vmem_limit_bytes=48 * 1024 * 1024
        ),
        name="layer",
    )(*operands)


def solution(mesh):
    placed = (
        P("seq", "ch"),
        P("seq", "ch"),
        P("seq", "ch"),
        P("seq", "ch"),
        P("ch"),
        P("ch", None),
        P("seq", "ch"),
    )
    return jax.shard_map(
        on_device,
        mesh=mesh,
        in_specs=placed,
        out_specs=(P("seq", "ch"), P("seq", "ch"), P("seq", "ch"), P("seq", "ch")),
        check_vma=False,
    )
```

```python
import functools
import math

import jax
import jax.numpy as jnp
import numpy as np
from jax import lax
from jax.experimental import pallas as pl
from jax.experimental.pallas import tpu as pltpu
from jax.sharding import PartitionSpec as P

F32 = jnp.float32
BF16 = jnp.bfloat16
MESH = pl.DeviceIdType.MESH

R = 128
L = R * R


def split_table(table):
    high = table.astype(np.float32).astype(jnp.bfloat16)
    low = (table - high.astype(np.float64)).astype(np.float32).astype(jnp.bfloat16)
    return high, low


def tables():
    n = np.arange(R, dtype=np.float64)
    p = n + 0.25
    first = np.exp(-2j * math.pi * np.outer(p, n) / R)
    turn = np.exp(-2j * math.pi * np.outer(p, n) / L)
    second = np.exp(-2j * math.pi * np.outer(n, n) / R)
    forward_a = np.concatenate([first.real, first.imag], axis=0)
    forward_b = np.block([[second.real, second.imag], [-second.imag, second.real]])
    inverse_b = forward_b.T
    inverse_a = np.concatenate([first.real.T, first.imag.T], axis=1) / L
    fa_high, fa_low = split_table(forward_a)
    fb_high, fb_low = split_table(forward_b)
    ib_high, ib_low = split_table(inverse_b)
    ia_high, ia_low = split_table(inverse_a)
    turns = np.stack([turn.real, turn.imag]).astype(np.float32)
    return (
        np.concatenate([fa_high, fa_low], axis=1),
        np.concatenate([fb_high, fb_high, fb_low], axis=0),
        np.concatenate([ib_high, ib_high, ib_low], axis=0),
        np.concatenate([ia_high, ia_high, ia_low], axis=1),
        np.concatenate([turns, turns], axis=2),
    )


def split(values):
    high = values.astype(BF16)
    low = (values - high.astype(F32)).astype(BF16)
    return high, low


def dot(left, right):
    return jnp.dot(left, right, preferred_element_type=F32)


TAPS, MIXED, CONV, GRAD, BACK = range(5)
COT_PAIR, COT_OWN, COT_FAR, GATED, WEIGHT, SIBLING, PARTIAL = range(7)


def layer_kernel(
    seq_count,
    ch_count,
    query_hbm,
    key_hbm,
    value_hbm,
    taps_hbm,
    skip_hbm,
    weight_hbm,
    out_grad,
    fa_hbm,
    fb_hbm,
    ib_hbm,
    ia_hbm,
    turn_hbm,
    mixed_out,
    query_grad,
    key_grad,
    value_grad,
    query,
    key,
    value,
    taps,
    skip,
    weight,
    fa,
    fb,
    ib,
    ia,
    turn,
    seq_send,
    seq_recv,
    stage,
    taps_spec,
    cotangents,
    gated_all,
    weight_cols,
    partial_send,
    partial_recv,
    grad_gated,
    grad_conv,
    seq_send_sem,
    seq_recv_sem,
    ch_send_sem,
    ch_recv_sem,
    local_sem,
):
    seq_me = lax.axis_index("seq")
    ch_me = lax.axis_index("ch")
    row_count, columns = query.shape
    blocks = row_count // R
    half = ch_count // 2
    pair = lax.rem(ch_me + half, ch_count)
    side = ch_me // half
    group = side * half
    spot = lax.rem(ch_me, half)
    core = lax.rem(seq_me, 2)
    sibling = seq_me + 1 - 2 * core

    barrier = pltpu.get_barrier_semaphore()

    def greet_seq(step, carry):
        peer = lax.rem(seq_me + step, seq_count)
        pl.semaphore_signal(barrier, inc=1, device_id={"seq": peer}, device_id_type=MESH)
        return carry

    lax.fori_loop(1, seq_count, greet_seq, 0)
    for step in range(1, half):
        peer = group + lax.rem(spot + step, half)
        pl.semaphore_signal(barrier, inc=1, device_id={"ch": peer}, device_id_type=MESH)
    pl.semaphore_signal(barrier, inc=1, device_id={"ch": pair}, device_id_type=MESH)

    fetches = [
        pltpu.make_async_copy(source, target, local_sem.at[index])
        for index, (source, target) in enumerate(
            (
                (taps_hbm, taps),
                (key_hbm, key),
                (value_hbm, value),
                (out_grad, cotangents.at[ch_me]),
                (fa_hbm, fa),
                (turn_hbm, turn),
                (fb_hbm, fb),
                (ib_hbm, ib),
                (ia_hbm, ia),
                (weight_hbm, weight),
                (query_hbm, query),
                (skip_hbm, skip),
            )
        )
    ]
    for fetch in fetches:
        fetch.start()

    def rows(block):
        return slice(block * R, (block + 1) * R)

    def lay_out(which, block, values):
        turned = jnp.transpose(values).astype(BF16)
        seq_send[which, :, block] = turned.reshape(seq_count, columns // seq_count, R)

    def exchange(which):
        def step(index, carry):
            peer = lax.rem(seq_me + index, seq_count)
            pltpu.make_async_remote_copy(
                src_ref=seq_send.at[which, peer],
                dst_ref=seq_recv.at[which, seq_me],
                send_sem=seq_send_sem.at[which],
                recv_sem=seq_recv_sem.at[which],
                device_id={"seq": peer},
                device_id_type=MESH,
            ).start()
            return carry

        lax.fori_loop(1, seq_count, step, 0)
        seq_recv[which, seq_me] = seq_send[which, seq_me]

    def exchanged(which):
        return pltpu.make_async_remote_copy(
            src_ref=seq_send.at[which, pl.ds(0, seq_count - 1)],
            dst_ref=seq_recv.at[which, pl.ds(0, seq_count - 1)],
            send_sem=seq_send_sem.at[which],
            recv_sem=seq_recv_sem.at[which],
            device_id={"seq": sibling},
            device_id_type=MESH,
        )

    def share(source, target, slot, which):
        for step in range(1, half):
            peer = group + lax.rem(spot + step, half)
            pltpu.make_async_remote_copy(
                src_ref=source,
                dst_ref=target.at[slot],
                send_sem=ch_send_sem.at[which],
                recv_sem=ch_recv_sem.at[which],
                device_id={"ch": peer},
                device_id_type=MESH,
            ).start()

    def shared(target, which):
        return pltpu.make_async_remote_copy(
            src_ref=target.at[pl.ds(0, half - 1)],
            dst_ref=target.at[pl.ds(0, half - 1)],
            send_sem=ch_send_sem.at[which],
            recv_sem=ch_recv_sem.at[which],
            device_id={"ch": pair},
            device_id_type=MESH,
        )

    def across(source, target, which):
        return pltpu.make_async_remote_copy(
            src_ref=source,
            dst_ref=target,
            send_sem=ch_send_sem.at[which],
            recv_sem=ch_recv_sem.at[which],
            device_id={"ch": pair},
            device_id_type=MESH,
        )

    def to_stage(which):
        stage[...] = seq_recv[which].astype(F32).reshape(L // R * 8, R)

    def from_stage(which):
        seq_send[which] = stage[...].astype(BF16).reshape(seq_count, blocks, 8, R)

    def spectrum(at):
        signal = jnp.concatenate(
            [stage[pl.ds(at + two, R, stride=8), :].astype(BF16) for two in range(2)], axis=1
        )
        both = dot(fa[...], jnp.concatenate([signal, signal], axis=0))
        real, imag = both[:R], both[R:]
        turned_re = real * turn[0] - imag * turn[1]
        turned_im = real * turn[1] + imag * turn[0]
        stacked = jnp.concatenate(
            [
                jnp.concatenate([turned_re[:, :R], turned_im[:, :R]], axis=1),
                jnp.concatenate([turned_re[:, R:], turned_im[:, R:]], axis=1),
            ],
            axis=0,
        )
        high, low = split(stacked)
        out = dot(jnp.concatenate([high, low, high], axis=1), fb[...])
        return out[:, :R], out[:, R:]

    def signal_of(real, imag, at):
        high, low = split(jnp.concatenate([real, imag], axis=1))
        back = dot(jnp.concatenate([high, low, high], axis=1), ib[...])
        real = jnp.concatenate([back[:R, :R], back[R:, :R]], axis=1)
        imag = jnp.concatenate([back[:R, R:], back[R:, R:]], axis=1)
        turned_re = real * turn[0] + imag * turn[1]
        turned_im = imag * turn[0] - real * turn[1]
        high, low = split(jnp.concatenate([turned_re, turned_im], axis=0))
        out = dot(ia[...], jnp.concatenate([high, low, high], axis=0))
        for two in range(2):
            stage[pl.ds(at + two, R, stride=8), :] = out[:, two * R : (two + 1) * R]

    def received(which, block):
        return jnp.transpose(seq_recv[which, :, block].astype(F32).reshape(columns, R))

    fetches[0].wait()
    for block in range(blocks):
        lay_out(TAPS, block, taps[rows(block), :])
    fetches[1].wait()
    fetches[2].wait()
    for block in range(blocks):
        lay_out(
            MIXED, block, key[rows(block), :].astype(F32) * value[rows(block), :].astype(F32)
        )

    pl.semaphore_wait(barrier, seq_count + half - 1)

    share(out_grad, cotangents, ch_me, COT_OWN)
    exchange(TAPS)
    across(out_grad, cotangents.at[ch_me], COT_PAIR).start()
    exchange(MIXED)

    for fetch in fetches[3:]:
        fetch.wait()

    exchanged(TAPS).wait_recv()
    to_stage(TAPS)

    across(out_grad, cotangents.at[pair], COT_PAIR).wait_recv()
    share(cotangents.at[pair], cotangents, pair, COT_FAR)

    def taps_step(index, carry):
        real, imag = spectrum(2 * index)
        taps_spec[index, :, :R] = real
        taps_spec[index, :, R:] = imag
        return carry

    lax.fori_loop(0, 4, taps_step, 0, unroll=True)

    exchanged(MIXED).wait_recv()
    to_stage(MIXED)

    def mixed_step(index, carry):
        real, imag = spectrum(2 * index)
        taps_re, taps_im = taps_spec[index, :, :R], taps_spec[index, :, R:]
        signal_of(real * taps_re - imag * taps_im, real * taps_im + imag * taps_re, 2 * index)
        return carry

    lax.fori_loop(0, 4, mixed_step, 0, unroll=True)
    from_stage(CONV)
    exchange(CONV)

    shared(cotangents, COT_OWN).wait_recv()
    shared(cotangents, COT_FAR).wait_recv()
    for block in range(blocks):
        total = None
        for source in range(ch_count):
            term = lax.dot_general(
                cotangents[source, rows(block), :],
                weight[:, source * columns : (source + 1) * columns],
                (((1,), (1,)), ((), ())),
                preferred_element_type=F32,
            )
            total = term if total is None else total + term
        grad_gated[rows(block), :] = total
        product = total * query[rows(block), :].astype(F32)
        grad_conv[rows(block), :] = product
        lay_out(GRAD, block, product)
    exchange(GRAD)

    half_rows = columns // 2
    for target in range(2):
        for step in range(1, half):
            to = lax.rem(spot + step, half)
            at = pl.multiple_of((target * half + to) * columns, columns)
            pltpu.make_async_remote_copy(
                src_ref=weight.at[
                    pl.ds(pl.multiple_of(core * half_rows, half_rows), half_rows),
                    pl.ds(at, columns),
                ],
                dst_ref=weight_cols.at[core, spot, target],
                send_sem=ch_send_sem.at[WEIGHT],
                recv_sem=ch_recv_sem.at[WEIGHT],
                device_id={"ch": group + to},
                device_id_type=MESH,
            ).start()
        at = pl.multiple_of((target * half + spot) * columns, columns)
        weight_cols[core, spot, target] = weight[
            pl.ds(pl.multiple_of(core * half_rows, half_rows), half_rows), pl.ds(at, columns)
        ]

    exchanged(CONV).wait_recv()
    gains = skip[...]
    for block in range(blocks):
        mixed = key[rows(block), :].astype(F32) * value[rows(block), :].astype(F32)
        conv = received(CONV, block) + gains * mixed
        gated_all[spot, rows(block), :] = (query[rows(block), :].astype(F32) * conv).astype(BF16)
        query_grad[rows(block), :] = (grad_gated[rows(block), :] * conv).astype(BF16)
    share(gated_all.at[spot], gated_all, spot, GATED)

    pltpu.make_async_remote_copy(
        src_ref=weight_cols.at[0, pl.ds(0, half - 1)],
        dst_ref=weight_cols.at[0, pl.ds(0, half - 1)],
        send_sem=ch_send_sem.at[WEIGHT],
        recv_sem=ch_recv_sem.at[WEIGHT],
        device_id={"ch": pair},
        device_id_type=MESH,
    ).wait()
    to_sibling = pltpu.make_async_remote_copy(
        src_ref=weight_cols.at[core],
        dst_ref=weight_cols.at[core],
        send_sem=ch_send_sem.at[SIBLING],
        recv_sem=ch_recv_sem.at[SIBLING],
        device_id={"seq": sibling},
        device_id_type=MESH,
    )
    to_sibling.start()

    exchanged(GRAD).wait_recv()
    to_stage(GRAD)

    def grad_step(index, carry):
        real, imag = spectrum(2 * index)
        taps_re, taps_im = taps_spec[index, :, :R], taps_spec[index, :, R:]
        signal_of(taps_re * real + taps_im * imag, taps_re * imag - taps_im * real, 2 * index)
        return carry

    lax.fori_loop(0, 4, grad_step, 0, unroll=True)
    from_stage(BACK)
    exchange(BACK)

    to_sibling.wait()
    shared(gated_all, GATED).wait_recv()

    def project(target, block):
        total = None
        for source in range(half):
            for part in range(2):
                term = dot(
                    gated_all[source, rows(block), part * half_rows : (part + 1) * half_rows],
                    weight_cols[part, source, target],
                )
                total = term if total is None else total + term
        return total

    for block in range(blocks):
        partial_send[rows(block), :] = project(1 - side, block).astype(BF16)
    across(partial_send, partial_recv, PARTIAL).start()

    exchanged(BACK).wait_recv()
    for block in range(blocks):
        total = received(BACK, block) + gains * grad_conv[rows(block), :]
        key_grad[rows(block), :] = (total * value[rows(block), :].astype(F32)).astype(BF16)
        value_grad[rows(block), :] = (total * key[rows(block), :].astype(F32)).astype(BF16)

    for block in range(blocks):
        grad_gated[rows(block), :] = project(side, block)
    across(partial_send, partial_recv, PARTIAL).wait()
    mixed_out[...] = (grad_gated[...] + partial_recv[...].astype(F32)).astype(BF16)

    for which in range(5):
        exchanged(which).wait_send()
    across(out_grad, cotangents.at[ch_me], COT_PAIR).wait_send()
    shared(cotangents, COT_OWN).wait_send()
    shared(cotangents, COT_FAR).wait_send()
    shared(gated_all, GATED).wait_send()


def hand_out_kernel(count, *refs):
    sources, targets, held = refs[:count], refs[count : 2 * count], refs[2 * count]
    into, out_of = refs[2 * count + 1 :]
    loads = [
        pltpu.make_async_copy(source, held.at[index], into.at[index])
        for index, source in enumerate(sources)
    ]
    stores = [
        pltpu.make_async_copy(held.at[index], target, out_of.at[index])
        for index, target in enumerate(targets)
    ]
    for load in loads:
        load.start()
    for load, store in zip(loads, stores):
        load.wait()
        store.start()
    for store in stores:
        store.wait()


def on_device(query_in, key_in, value_in, filter_taps, skip_gain, out_weight, out_grad):
    seq_count = lax.axis_size("seq")
    ch_count = lax.axis_size("ch")
    row_count, columns = query_in.shape
    blocks = row_count // R
    half = ch_count // 2
    constants = tuple(jnp.asarray(table) for table in tables())
    operands = (
        query_in,
        key_in,
        value_in,
        filter_taps,
        skip_gain.reshape(1, columns),
        out_weight,
        out_grad,
    ) + constants
    in_hbm = pl.BlockSpec(memory_space=pltpu.HBM)
    in_vmem = pl.BlockSpec(memory_space=pltpu.VMEM)
    block_shape = (row_count, columns)
    results = pl.pallas_call(
        functools.partial(layer_kernel, seq_count, ch_count),
        out_shape=[jax.ShapeDtypeStruct(block_shape, BF16)] * 4,
        in_specs=[in_hbm] * len(operands),
        out_specs=[in_vmem] * 4,
        scratch_shapes=[
            pltpu.VMEM(block_shape, BF16),
            pltpu.VMEM(block_shape, BF16),
            pltpu.VMEM(block_shape, BF16),
            pltpu.VMEM(block_shape, F32),
            pltpu.VMEM((1, columns), F32),
            pltpu.VMEM(out_weight.shape, BF16),
        ]
        + [pltpu.VMEM(table.shape, table.dtype) for table in constants]
        + [
            pltpu.VMEM((5, seq_count, blocks, 8, R), BF16),
            pltpu.VMEM((5, seq_count, blocks, 8, R), BF16),
            pltpu.VMEM((L // R * 8, R), F32),
            pltpu.VMEM((4, 2 * R, 2 * R), F32),
            pltpu.VMEM((ch_count, row_count, columns), BF16),
            pltpu.VMEM((half, row_count, columns), BF16),
            pltpu.VMEM((2, half, 2, columns // 2, columns), BF16),
            pltpu.VMEM(block_shape, BF16),
            pltpu.VMEM(block_shape, BF16),
            pltpu.VMEM(block_shape, F32),
            pltpu.VMEM(block_shape, F32),
            pltpu.SemaphoreType.DMA((5,)),
            pltpu.SemaphoreType.DMA((5,)),
            pltpu.SemaphoreType.DMA((7,)),
            pltpu.SemaphoreType.DMA((7,)),
            pltpu.SemaphoreType.DMA((12,)),
        ],
        compiler_params=pltpu.CompilerParams(
            collective_id=0, has_side_effects=True, vmem_limit_bytes=56 * 1024 * 1024
        ),
        name="layer",
    )(*operands)
    return pl.pallas_call(
        functools.partial(hand_out_kernel, len(results)),
        out_shape=[jax.ShapeDtypeStruct(block_shape, BF16)] * 4,
        in_specs=[in_hbm] * 4,
        out_specs=[in_hbm] * 4,
        scratch_shapes=[
            pltpu.VMEM((4,) + block_shape, BF16),
            pltpu.SemaphoreType.DMA((4,)),
            pltpu.SemaphoreType.DMA((4,)),
        ],
        compiler_params=pltpu.CompilerParams(vmem_limit_bytes=56 * 1024 * 1024),
        name="hand_out",
    )(*results)


def solution(mesh):
    placed = (
        P("seq", "ch"),
        P("seq", "ch"),
        P("seq", "ch"),
        P("seq", "ch"),
        P("ch"),
        P("ch", None),
        P("seq", "ch"),
    )
    return jax.shard_map(
        on_device,
        mesh=mesh,
        in_specs=placed,
        out_specs=(P("seq", "ch"), P("seq", "ch"), P("seq", "ch"), P("seq", "ch")),
        check_vma=False,
    )
```

```python
import functools
import math

import jax
import jax.numpy as jnp
import numpy as np
from jax import lax
from jax.experimental import pallas as pl
from jax.experimental.pallas import tpu as pltpu
from jax.sharding import PartitionSpec as P

F32 = jnp.float32
BF16 = jnp.bfloat16
MESH = pl.DeviceIdType.MESH

R = 128
L = R * R


def split_table(table):
    high = table.astype(np.float32).astype(jnp.bfloat16)
    low = (table - high.astype(np.float64)).astype(np.float32).astype(jnp.bfloat16)
    return high, low


def tables():
    n = np.arange(R, dtype=np.float64)
    p = n + 0.25
    first = np.exp(-2j * math.pi * np.outer(p, n) / R)
    turn = np.exp(-2j * math.pi * np.outer(p, n) / L)
    second = np.exp(-2j * math.pi * np.outer(n, n) / R)
    forward_a = np.concatenate([first.real, first.imag], axis=0)
    forward_b = np.block([[second.real, second.imag], [-second.imag, second.real]])
    inverse_b = forward_b.T
    inverse_a = np.concatenate([first.real.T, first.imag.T], axis=1) / L
    fa_high, fa_low = split_table(forward_a)
    fb_high, fb_low = split_table(forward_b)
    ib_high, ib_low = split_table(inverse_b)
    ia_high, ia_low = split_table(inverse_a)
    turns = np.stack([turn.real, turn.imag]).astype(np.float32)
    return (
        np.concatenate([fa_high, fa_low], axis=1),
        np.concatenate([fb_high, fb_high, fb_low], axis=0),
        np.concatenate([ib_high, ib_high, ib_low], axis=0),
        np.concatenate([ia_high, ia_high, ia_low], axis=1),
        np.concatenate([turns, turns], axis=2),
    )


def split(values):
    high = values.astype(BF16)
    low = (values - high.astype(F32)).astype(BF16)
    return high, low


def dot(left, right):
    return jnp.dot(left, right, preferred_element_type=F32)


TAPS, MIXED, CONV, GRAD, BACK = range(5)
COT_PAIR, COT_OWN, COT_OWN_ON, COT_FAR, COT_FAR_ON, GATED, GATED_ON, PARTIAL = range(0, 16, 2)
WEIGHT, SIBLING = 16, 17
PARTS = 2


def layer_kernel(
    seq_count,
    ch_count,
    query_hbm,
    key_hbm,
    value_hbm,
    taps_hbm,
    skip_hbm,
    weight_hbm,
    out_grad,
    fa_hbm,
    fb_hbm,
    ib_hbm,
    ia_hbm,
    turn_hbm,
    mixed_out,
    query_grad,
    key_grad,
    value_grad,
    query,
    key,
    value,
    taps,
    skip,
    weight,
    fa,
    fb,
    ib,
    ia,
    turn,
    seq_send,
    seq_recv,
    stage,
    taps_spec,
    cotangents,
    gated_all,
    weight_cols,
    partial_send,
    partial_recv,
    grad_gated,
    grad_conv,
    seq_send_sem,
    seq_recv_sem,
    ch_send_sem,
    ch_recv_sem,
    local_sem,
):
    seq_me = lax.axis_index("seq")
    ch_me = lax.axis_index("ch")
    row_count, columns = query.shape
    blocks = row_count // R
    half = ch_count // 2
    pair = lax.rem(ch_me + half, ch_count)
    side = ch_me // half
    group = side * half
    spot = lax.rem(ch_me, half)
    core = lax.rem(seq_me, 2)
    sibling = seq_me + 1 - 2 * core
    far_group = half - group
    turn_up = lax.rem(spot + 1, half)
    turn_down = lax.rem(spot + half - 1, half)
    per_part = blocks // PARTS
    part_rows = row_count // PARTS

    barrier = pltpu.get_barrier_semaphore()

    def greet_seq(step, carry):
        peer = lax.rem(seq_me + step, seq_count)
        pl.semaphore_signal(barrier, inc=1, device_id={"seq": peer}, device_id_type=MESH)
        return carry

    lax.fori_loop(1, seq_count, greet_seq, 0)
    for step in range(1, half):
        peer = group + lax.rem(spot + step, half)
        pl.semaphore_signal(barrier, inc=1, device_id={"ch": peer}, device_id_type=MESH)
    pl.semaphore_signal(barrier, inc=1, device_id={"ch": pair}, device_id_type=MESH)

    fetches = [
        pltpu.make_async_copy(source, target, local_sem.at[index])
        for index, (source, target) in enumerate(
            (
                (taps_hbm, taps),
                (key_hbm, key),
                (value_hbm, value),
                (out_grad, cotangents.at[ch_me]),
                (fa_hbm, fa),
                (turn_hbm, turn),
                (fb_hbm, fb),
                (ib_hbm, ib),
                (ia_hbm, ia),
                (weight_hbm, weight),
                (query_hbm, query),
                (skip_hbm, skip),
            )
        )
    ]
    for fetch in fetches:
        fetch.start()

    def rows(block):
        return slice(block * R, (block + 1) * R)

    def lay_out(which, block, values):
        turned = jnp.transpose(values).astype(BF16)
        seq_send[which, :, block] = turned.reshape(seq_count, columns // seq_count, R)

    def exchange(which, part=None):
        span = pl.ds(0, blocks) if part is None else pl.ds(part * per_part, per_part)
        sem = 2 * which + (0 if part is None else part)

        def step(index, carry):
            peer = lax.rem(seq_me + index, seq_count)
            pltpu.make_async_remote_copy(
                src_ref=seq_send.at[which, peer, span],
                dst_ref=seq_recv.at[which, seq_me, span],
                send_sem=seq_send_sem.at[sem],
                recv_sem=seq_recv_sem.at[sem],
                device_id={"seq": peer},
                device_id_type=MESH,
            ).start()
            return carry

        lax.fori_loop(1, seq_count, step, 0)
        seq_recv[which, seq_me, span] = seq_send[which, seq_me, span]

    def exchanged(which, part=None):
        span = pl.ds(0, blocks) if part is None else pl.ds(part * per_part, per_part)
        sem = 2 * which + (0 if part is None else part)
        return pltpu.make_async_remote_copy(
            src_ref=seq_send.at[which, pl.ds(0, seq_count - 1), span],
            dst_ref=seq_recv.at[which, pl.ds(0, seq_count - 1), span],
            send_sem=seq_send_sem.at[sem],
            recv_sem=seq_recv_sem.at[sem],
            device_id={"seq": sibling},
            device_id_type=MESH,
        )

    def tokens(part):
        return pl.ds(part * part_rows, part_rows)

    def ring(source, target, slot, which, part):
        for to in (turn_up, turn_down):
            pltpu.make_async_remote_copy(
                src_ref=source.at[tokens(part)],
                dst_ref=target.at[slot, tokens(part)],
                send_sem=ch_send_sem.at[which + part],
                recv_sem=ch_recv_sem.at[which + part],
                device_id={"ch": group + to},
                device_id_type=MESH,
            ).start()

    def ring_done(target, which, part):
        return pltpu.make_async_remote_copy(
            src_ref=target.at[pl.ds(0, 2), tokens(part)],
            dst_ref=target.at[pl.ds(0, 2), tokens(part)],
            send_sem=ch_send_sem.at[which + part],
            recv_sem=ch_recv_sem.at[which + part],
            device_id={"ch": pair},
            device_id_type=MESH,
        )

    def opposite(source, target, slot, which, part):
        pltpu.make_async_remote_copy(
            src_ref=source.at[tokens(part)],
            dst_ref=target.at[slot, tokens(part)],
            send_sem=ch_send_sem.at[which + part],
            recv_sem=ch_recv_sem.at[which + part],
            device_id={"ch": group + lax.rem(spot + 2, half)},
            device_id_type=MESH,
        ).start()

    def ring3_done(part, target=None, which=GATED):
        target = gated_all if target is None else target
        return pltpu.make_async_remote_copy(
            src_ref=target.at[pl.ds(0, 3), tokens(part)],
            dst_ref=target.at[pl.ds(0, 3), tokens(part)],
            send_sem=ch_send_sem.at[which + part],
            recv_sem=ch_recv_sem.at[which + part],
            device_id={"ch": pair},
            device_id_type=MESH,
        )

    def hand_on(target, base, which, part):
        for index, (origin, to) in enumerate(((turn_down, turn_up), (turn_up, turn_down))):
            piece = pl.ds((part * per_part + index) * R, R)
            pltpu.make_async_remote_copy(
                src_ref=target.at[base + origin, piece],
                dst_ref=target.at[base + origin, piece],
                send_sem=ch_send_sem.at[which + part],
                recv_sem=ch_recv_sem.at[which + part],
                device_id={"ch": group + to},
                device_id_type=MESH,
            ).start()

    def hand_on_done(target, which, part):
        return pltpu.make_async_remote_copy(
            src_ref=target.at[0, tokens(part)],
            dst_ref=target.at[0, tokens(part)],
            send_sem=ch_send_sem.at[which + part],
            recv_sem=ch_recv_sem.at[which + part],
            device_id={"ch": pair},
            device_id_type=MESH,
        )

    def across(source, target, which, part):
        return pltpu.make_async_remote_copy(
            src_ref=source.at[tokens(part)],
            dst_ref=target.at[tokens(part)],
            send_sem=ch_send_sem.at[which + part],
            recv_sem=ch_recv_sem.at[which + part],
            device_id={"ch": pair},
            device_id_type=MESH,
        )

    def to_stage(which):
        stage[...] = seq_recv[which].astype(F32).reshape(L // R * 8, R)

    def from_stage(which):
        seq_send[which] = stage[...].astype(BF16).reshape(seq_count, blocks, 8, R)

    def spectrum(at):
        signal = jnp.concatenate(
            [stage[pl.ds(at + two, R, stride=8), :].astype(BF16) for two in range(2)], axis=1
        )
        both = dot(fa[...], jnp.concatenate([signal, signal], axis=0))
        real, imag = both[:R], both[R:]
        turned_re = real * turn[0] - imag * turn[1]
        turned_im = real * turn[1] + imag * turn[0]
        stacked = jnp.concatenate(
            [
                jnp.concatenate([turned_re[:, :R], turned_im[:, :R]], axis=1),
                jnp.concatenate([turned_re[:, R:], turned_im[:, R:]], axis=1),
            ],
            axis=0,
        )
        high, low = split(stacked)
        out = dot(jnp.concatenate([high, low, high], axis=1), fb[...])
        return out[:, :R], out[:, R:]

    def signal_of(real, imag, at):
        high, low = split(jnp.concatenate([real, imag], axis=1))
        back = dot(jnp.concatenate([high, low, high], axis=1), ib[...])
        real = jnp.concatenate([back[:R, :R], back[R:, :R]], axis=1)
        imag = jnp.concatenate([back[:R, R:], back[R:, R:]], axis=1)
        turned_re = real * turn[0] + imag * turn[1]
        turned_im = imag * turn[0] - real * turn[1]
        high, low = split(jnp.concatenate([turned_re, turned_im], axis=0))
        out = dot(ia[...], jnp.concatenate([high, low, high], axis=0))
        for two in range(2):
            stage[pl.ds(at + two, R, stride=8), :] = out[:, two * R : (two + 1) * R]

    def received(which, block):
        return jnp.transpose(seq_recv[which, :, block].astype(F32).reshape(columns, R))

    fetches[0].wait()
    for block in range(blocks):
        lay_out(TAPS, block, taps[rows(block), :])

    pl.semaphore_wait(barrier, seq_count + half - 1)

    ring(out_grad, cotangents, ch_me, COT_OWN, 0)
    across(out_grad, cotangents.at[ch_me], COT_PAIR, 0).start()
    exchange(TAPS)
    ring(out_grad, cotangents, ch_me, COT_OWN, 1)
    across(out_grad, cotangents.at[ch_me], COT_PAIR, 1).start()
    fetches[1].wait()
    fetches[2].wait()
    for block in range(blocks):
        lay_out(
            MIXED, block, key[rows(block), :].astype(F32) * value[rows(block), :].astype(F32)
        )
    exchange(MIXED)

    for fetch in fetches[3:]:
        fetch.wait()

    def cotangent_pair(part):
        across(out_grad, cotangents.at[pair], COT_PAIR, part).wait_recv()
        ring(cotangents.at[pair], cotangents, pair, COT_FAR, part)
        if part in (0, 1):
            opposite(cotangents.at[pair], cotangents, pair, COT_FAR, part)

    def cotangent_own_on(part):
        ring_done(cotangents, COT_OWN, part).wait_recv()
        hand_on(cotangents, group, COT_OWN_ON, part)

    def cotangent_far_on(part):
        ring_done(cotangents, COT_FAR, part).wait_recv()
        hand_on(cotangents, far_group, COT_FAR_ON, part)

    cotangent_own_on(0)
    cotangent_pair(0)
    cotangent_own_on(1)

    cotangent_pair(1)
    exchanged(TAPS).wait_recv()
    to_stage(TAPS)

    def taps_step(index, carry):
        real, imag = spectrum(2 * index)
        taps_spec[index, :, :R] = real
        taps_spec[index, :, R:] = imag
        return carry

    lax.fori_loop(0, 4, taps_step, 0, unroll=True)

    exchanged(MIXED).wait_recv()
    to_stage(MIXED)

    def mixed_step(index, carry):
        real, imag = spectrum(2 * index)
        taps_re, taps_im = taps_spec[index, :, :R], taps_spec[index, :, R:]
        signal_of(real * taps_re - imag * taps_im, real * taps_im + imag * taps_re, 2 * index)
        return carry

    lax.fori_loop(0, 4, mixed_step, 0, unroll=True)
    from_stage(CONV)
    exchange(CONV, 0)
    exchange(CONV, 1)

    for part in range(PARTS):
        hand_on_done(cotangents, COT_OWN_ON, part).wait_recv()
        if part in (0, 1):
            ring3_done(part, cotangents, COT_FAR).wait_recv()
        else:
            hand_on_done(cotangents, COT_FAR_ON, part).wait_recv()
        for block in range(part * per_part, (part + 1) * per_part):
            total = None
            for source in range(ch_count):
                term = lax.dot_general(
                    cotangents[source, rows(block), :],
                    weight[:, source * columns : (source + 1) * columns],
                    (((1,), (1,)), ((), ())),
                    preferred_element_type=F32,
                )
                total = term if total is None else total + term
            grad_gated[rows(block), :] = total
            product = total * query[rows(block), :].astype(F32)
            grad_conv[rows(block), :] = product
            lay_out(GRAD, block, product)
        exchange(GRAD, part)

    half_rows = columns // 2
    for target in range(2):
        for step in range(1, half):
            to = lax.rem(spot + step, half)
            at = pl.multiple_of((target * half + to) * columns, columns)
            pltpu.make_async_remote_copy(
                src_ref=weight.at[
                    pl.ds(pl.multiple_of(core * half_rows, half_rows), half_rows),
                    pl.ds(at, columns),
                ],
                dst_ref=weight_cols.at[core, spot, target],
                send_sem=ch_send_sem.at[WEIGHT],
                recv_sem=ch_recv_sem.at[WEIGHT],
                device_id={"ch": group + to},
                device_id_type=MESH,
            ).start()
        at = pl.multiple_of((target * half + spot) * columns, columns)
        weight_cols[core, spot, target] = weight[
            pl.ds(pl.multiple_of(core * half_rows, half_rows), half_rows), pl.ds(at, columns)
        ]

    gains = skip[...]
    for part in range(PARTS):
        exchanged(CONV, part).wait_recv()
        for block in range(part * per_part, (part + 1) * per_part):
            mixed = key[rows(block), :].astype(F32) * value[rows(block), :].astype(F32)
            conv = received(CONV, block) + gains * mixed
            gated_all[spot, rows(block), :] = (query[rows(block), :].astype(F32) * conv).astype(
                BF16
            )
            query_grad[rows(block), :] = (grad_gated[rows(block), :] * conv).astype(BF16)
        ring(gated_all.at[spot], gated_all, spot, GATED, part)
        pltpu.make_async_remote_copy(
            src_ref=gated_all.at[spot, tokens(part)],
            dst_ref=gated_all.at[spot, tokens(part)],
            send_sem=ch_send_sem.at[GATED + part],
            recv_sem=ch_recv_sem.at[GATED + part],
            device_id={"ch": group + lax.rem(spot + 2, half)},
            device_id_type=MESH,
        ).start()

    pltpu.make_async_remote_copy(
        src_ref=weight_cols.at[0, pl.ds(0, half - 1)],
        dst_ref=weight_cols.at[0, pl.ds(0, half - 1)],
        send_sem=ch_send_sem.at[WEIGHT],
        recv_sem=ch_recv_sem.at[WEIGHT],
        device_id={"ch": pair},
        device_id_type=MESH,
    ).wait()
    to_sibling = pltpu.make_async_remote_copy(
        src_ref=weight_cols.at[core],
        dst_ref=weight_cols.at[core],
        send_sem=ch_send_sem.at[SIBLING],
        recv_sem=ch_recv_sem.at[SIBLING],
        device_id={"seq": sibling},
        device_id_type=MESH,
    )
    to_sibling.start()


    exchanged(GRAD, 0).wait_recv()
    exchanged(GRAD, 1).wait_recv()
    to_stage(GRAD)

    def grad_step(index, carry):
        real, imag = spectrum(2 * index)
        taps_re, taps_im = taps_spec[index, :, :R], taps_spec[index, :, R:]
        signal_of(taps_re * real + taps_im * imag, taps_re * imag - taps_im * real, 2 * index)
        return carry

    lax.fori_loop(0, 4, grad_step, 0, unroll=True)
    from_stage(BACK)
    exchange(BACK, 0)
    exchange(BACK, 1)


    to_sibling.wait()

    def project(target, block):
        total = None
        for source in range(half):
            for part in range(2):
                term = dot(
                    gated_all[source, rows(block), part * half_rows : (part + 1) * half_rows],
                    weight_cols[part, source, target],
                )
                total = term if total is None else total + term
        return total

    for part in range(PARTS):
        ring3_done(part).wait_recv()
        for block in range(part * per_part, (part + 1) * per_part):
            partial_send[rows(block), :] = project(1 - side, block).astype(BF16)
        across(partial_send, partial_recv, PARTIAL, part).start()
        for block in range(part * per_part, (part + 1) * per_part):
            grad_gated[rows(block), :] = project(side, block)

    for part in range(PARTS):
        exchanged(BACK, part).wait_recv()
        for block in range(part * per_part, (part + 1) * per_part):
            total = received(BACK, block) + gains * grad_conv[rows(block), :]
            key_grad[rows(block), :] = (total * value[rows(block), :].astype(F32)).astype(BF16)
            value_grad[rows(block), :] = (total * key[rows(block), :].astype(F32)).astype(BF16)

    for part in range(PARTS):
        across(partial_send, partial_recv, PARTIAL, part).wait_recv()
        for block in range(part * per_part, (part + 1) * per_part):
            mixed_out[rows(block), :] = (
                grad_gated[rows(block), :] + partial_recv[rows(block), :].astype(F32)
            ).astype(BF16)

    exchanged(TAPS).wait_send()
    exchanged(MIXED).wait_send()
    for part in range(PARTS):
        for which in (CONV, GRAD, BACK):
            exchanged(which, part).wait_send()
        across(out_grad, cotangents.at[ch_me], COT_PAIR, part).wait_send()
        across(partial_send, partial_recv, PARTIAL, part).wait_send()
        ring_done(cotangents, COT_OWN, part).wait_send()
        hand_on_done(cotangents, COT_OWN_ON, part).wait_send()
        if part in (0, 1):
            ring3_done(part, cotangents, COT_FAR).wait_send()
        else:
            ring_done(cotangents, COT_FAR, part).wait_send()
            hand_on_done(cotangents, COT_FAR_ON, part).wait_send()
        ring3_done(part).wait_send()


def hand_out_kernel(count, *refs):
    sources, targets, sem = refs[:count], refs[count : 2 * count], refs[2 * count]
    copies = [
        pltpu.make_async_copy(source, target, sem.at[index])
        for index, (source, target) in enumerate(zip(sources, targets))
    ]
    for copy in copies:
        copy.start()
    for copy in copies:
        copy.wait()


def on_device(query_in, key_in, value_in, filter_taps, skip_gain, out_weight, out_grad):
    seq_count = lax.axis_size("seq")
    ch_count = lax.axis_size("ch")
    row_count, columns = query_in.shape
    blocks = row_count // R
    half = ch_count // 2
    constants = tuple(jnp.asarray(table) for table in tables())
    operands = (
        query_in,
        key_in,
        value_in,
        filter_taps,
        skip_gain.reshape(1, columns),
        out_weight,
        out_grad,
    ) + constants
    operands = tuple(pltpu.with_memory_space_constraint(each, pltpu.HBM) for each in operands)
    in_hbm = pl.BlockSpec(memory_space=pltpu.HBM)
    in_vmem = pl.BlockSpec(memory_space=pltpu.VMEM)
    block_shape = (row_count, columns)
    results = pl.pallas_call(
        functools.partial(layer_kernel, seq_count, ch_count),
        out_shape=[jax.ShapeDtypeStruct(block_shape, BF16)] * 4,
        in_specs=[in_hbm] * len(operands),
        out_specs=[in_vmem] * 4,
        scratch_shapes=[
            pltpu.VMEM(block_shape, BF16),
            pltpu.VMEM(block_shape, BF16),
            pltpu.VMEM(block_shape, BF16),
            pltpu.VMEM(block_shape, F32),
            pltpu.VMEM((1, columns), F32),
            pltpu.VMEM(out_weight.shape, BF16),
        ]
        + [pltpu.VMEM(table.shape, table.dtype) for table in constants]
        + [
            pltpu.VMEM((5, seq_count, blocks, 8, R), BF16),
            pltpu.VMEM((5, seq_count, blocks, 8, R), BF16),
            pltpu.VMEM((L // R * 8, R), F32),
            pltpu.VMEM((4, 2 * R, 2 * R), F32),
            pltpu.VMEM((ch_count, row_count, columns), BF16),
            pltpu.VMEM((half, row_count, columns), BF16),
            pltpu.VMEM((2, half, 2, columns // 2, columns), BF16),
            pltpu.VMEM(block_shape, BF16),
            pltpu.VMEM(block_shape, BF16),
            pltpu.VMEM(block_shape, F32),
            pltpu.VMEM(block_shape, F32),
            pltpu.SemaphoreType.DMA((10,)),
            pltpu.SemaphoreType.DMA((10,)),
            pltpu.SemaphoreType.DMA((18,)),
            pltpu.SemaphoreType.DMA((18,)),
            pltpu.SemaphoreType.DMA((12,)),
        ],
        compiler_params=pltpu.CompilerParams(
            collective_id=0, has_side_effects=True, vmem_limit_bytes=48 * 1024 * 1024
        ),
        name="layer",
    )(*operands)
    return pl.pallas_call(
        functools.partial(hand_out_kernel, len(results)),
        out_shape=[jax.ShapeDtypeStruct(block_shape, BF16)] * 4,
        in_specs=[in_vmem] * 4,
        out_specs=[in_hbm] * 4,
        scratch_shapes=[pltpu.SemaphoreType.DMA((4,))],
        name="hand_out",
    )(*[pltpu.with_memory_space_constraint(each, pltpu.VMEM) for each in results])


def solution(mesh):
    placed = (
        P("seq", "ch"),
        P("seq", "ch"),
        P("seq", "ch"),
        P("seq", "ch"),
        P("ch"),
        P("ch", None),
        P("seq", "ch"),
    )
    return jax.shard_map(
        on_device,
        mesh=mesh,
        in_specs=placed,
        out_specs=(P("seq", "ch"), P("seq", "ch"), P("seq", "ch"), P("seq", "ch")),
        check_vma=False,
    )
```

```python
import functools
import math

import jax
import jax.numpy as jnp
import numpy as np
from jax import lax
from jax.experimental import pallas as pl
from jax.experimental.pallas import tpu as pltpu
from jax.sharding import PartitionSpec as P

F32 = jnp.float32
BF16 = jnp.bfloat16
MESH = pl.DeviceIdType.MESH

R = 128
L = R * R


def split_table(table):
    high = table.astype(np.float32).astype(jnp.bfloat16)
    low = (table - high.astype(np.float64)).astype(np.float32).astype(jnp.bfloat16)
    return high, low


def tables():
    n = np.arange(R, dtype=np.float64)
    p = n + 0.25
    first = np.exp(-2j * math.pi * np.outer(p, n) / R)
    turn = np.exp(-2j * math.pi * np.outer(p, n) / L)
    second = np.exp(-2j * math.pi * np.outer(n, n) / R)
    place = np.arange(R)
    order = 4 * (place % 64 // 2) + 2 * (place // 64) + place % 2
    first = first[:, order]
    forward_a = np.concatenate([first.real, first.imag], axis=0)
    forward_b = np.block([[second.real, second.imag], [-second.imag, second.real]])
    inverse_b = forward_b.T
    inverse_a = np.concatenate([first.real.T, first.imag.T], axis=1) / L
    fa_high, fa_low = split_table(forward_a)
    fb_high, fb_low = split_table(forward_b)
    ib_high, ib_low = split_table(inverse_b)
    ia_high, ia_low = split_table(inverse_a)
    turns = np.stack([turn.real, turn.imag]).astype(np.float32)
    return (
        np.concatenate([fa_high, fa_low], axis=1),
        np.concatenate([fb_high, fb_high, fb_low], axis=0),
        np.concatenate([ib_high, ib_high, ib_low], axis=0),
        np.concatenate([ia_high, ia_high, ia_low], axis=1),
        np.concatenate([turns, turns], axis=2),
    )


def split(values):
    high = values.astype(BF16)
    low = (values - high.astype(F32)).astype(BF16)
    return high, low


def dot(left, right):
    return jnp.dot(left, right, preferred_element_type=F32)


TAPS, MIXED, CONV, GRAD, BACK = range(5)
COT_PAIR, COT_OWN, COT_OWN_ON, COT_FAR = range(0, 8, 2)
WEIGHT, SIBLING, GATED, PARTIAL = 8, 9, 10, 14
PARTS = 2


def layer_kernel(
    seq_count,
    ch_count,
    query_hbm,
    key_hbm,
    value_hbm,
    taps_hbm,
    skip_hbm,
    weight_hbm,
    out_grad,
    fa_hbm,
    fb_hbm,
    ib_hbm,
    ia_hbm,
    turn_hbm,
    mixed_out,
    query_grad,
    key_grad,
    value_grad,
    query,
    key,
    value,
    taps,
    skip,
    weight,
    fa,
    fb,
    ib,
    ia,
    turn,
    seq_send,
    seq_recv,
    spread_out,
    spread_in,
    stage_taps,
    stage,
    taps_spec,
    cotangents,
    gated_all,
    weight_cols,
    partial_send,
    partial_recv,
    grad_gated,
    grad_conv,
    seq_send_sem,
    seq_recv_sem,
    ch_send_sem,
    ch_recv_sem,
    local_sem,
):
    seq_me = lax.axis_index("seq")
    ch_me = lax.axis_index("ch")
    row_count, columns = query.shape
    blocks = row_count // R
    half = ch_count // 2
    pair = lax.rem(ch_me + half, ch_count)
    side = ch_me // half
    group = side * half
    spot = lax.rem(ch_me, half)
    core = lax.rem(seq_me, 2)
    sibling = seq_me + 1 - 2 * core
    turn_up = lax.rem(spot + 1, half)
    turn_down = lax.rem(spot + half - 1, half)
    per_part = blocks // PARTS
    part_rows = row_count // PARTS

    barrier = pltpu.get_barrier_semaphore()

    def greet_seq(step, carry):
        peer = lax.rem(seq_me + step, seq_count)
        pl.semaphore_signal(barrier, inc=1, device_id={"seq": peer}, device_id_type=MESH)
        return carry

    lax.fori_loop(1, seq_count, greet_seq, 0)
    for step in range(1, half):
        peer = group + lax.rem(spot + step, half)
        pl.semaphore_signal(barrier, inc=1, device_id={"ch": peer}, device_id_type=MESH)
    pl.semaphore_signal(barrier, inc=1, device_id={"ch": pair}, device_id_type=MESH)

    fetches = [
        pltpu.make_async_copy(source, target, local_sem.at[index])
        for index, (source, target) in enumerate(
            (
                (taps_hbm, taps),
                (key_hbm, key),
                (value_hbm, value),
                (out_grad, cotangents.at[ch_me]),
                (fa_hbm, fa),
                (turn_hbm, turn),
                (fb_hbm, fb),
                (ib_hbm, ib),
                (ia_hbm, ia),
                (weight_hbm, weight),
                (query_hbm, query),
                (skip_hbm, skip),
            )
        )
    ]
    for fetch in fetches:
        fetch.start()

    def rows(block):
        return slice(block * R, (block + 1) * R)

    width = columns // 2
    each = width // seq_count

    def lay_out(block, values):
        part, at = block // per_part, block % per_part
        for h in range(2):
            turned = jnp.transpose(values[:, h * width : (h + 1) * width])
            for j in range(each):
                spread_out[
                    h, part, pl.ds(each * at + j, seq_count, stride=each * per_part), :
                ] = turned[seq_count * j : seq_count * (j + 1)]

    def laid_out(which, h, part):
        seq_send[which, h, :, part] = (
            spread_out[h, part].astype(BF16).reshape(seq_count, each * per_part, R)
        )

    def span_of(h, part):
        halves = pl.ds(0, 2) if h is None else pl.ds(h, 1)
        parts = pl.ds(0, PARTS) if part is None else pl.ds(part, 1)
        return halves, parts

    def exchange(which, sem, h=None, part=None):
        halves, parts = span_of(h, part)

        def step(index, carry):
            peer = lax.rem(seq_me + index, seq_count)
            pltpu.make_async_remote_copy(
                src_ref=seq_send.at[which, halves, peer, parts],
                dst_ref=seq_recv.at[which, halves, seq_me, parts],
                send_sem=seq_send_sem.at[3 * which + sem],
                recv_sem=seq_recv_sem.at[3 * which + sem],
                device_id={"seq": peer},
                device_id_type=MESH,
            ).start()
            return carry

        lax.fori_loop(1, seq_count, step, 0)
        for one_h in (0, 1) if h is None else (h,):
            for one_part in range(PARTS) if part is None else (part,):
                seq_recv[which, one_h, seq_me, one_part] = seq_send[
                    which, one_h, seq_me, one_part
                ]

    def exchanged(which, sem, h=None, part=None):
        halves, parts = span_of(h, part)
        return pltpu.make_async_remote_copy(
            src_ref=seq_send.at[which, halves, pl.ds(0, seq_count - 1), parts],
            dst_ref=seq_recv.at[which, halves, pl.ds(0, seq_count - 1), parts],
            send_sem=seq_send_sem.at[3 * which + sem],
            recv_sem=seq_recv_sem.at[3 * which + sem],
            device_id={"seq": sibling},
            device_id_type=MESH,
        )

    def tokens(part):
        return pl.ds(part * part_rows, part_rows)

    def ring(source, target, slot, which, part):
        for to in (turn_up, turn_down):
            pltpu.make_async_remote_copy(
                src_ref=source.at[tokens(part)],
                dst_ref=target.at[slot, tokens(part)],
                send_sem=ch_send_sem.at[which + part],
                recv_sem=ch_recv_sem.at[which + part],
                device_id={"ch": group + to},
                device_id_type=MESH,
            ).start()

    def ring_done(target, which, part):
        return pltpu.make_async_remote_copy(
            src_ref=target.at[pl.ds(0, 2), tokens(part)],
            dst_ref=target.at[pl.ds(0, 2), tokens(part)],
            send_sem=ch_send_sem.at[which + part],
            recv_sem=ch_recv_sem.at[which + part],
            device_id={"ch": pair},
            device_id_type=MESH,
        )

    def gated_out_to(block):
        for step in (1, half - 1, 2):
            pltpu.make_async_remote_copy(
                src_ref=gated_all.at[spot, pl.ds(block * R, R)],
                dst_ref=gated_all.at[spot, pl.ds(block * R, R)],
                send_sem=ch_send_sem.at[GATED + block],
                recv_sem=ch_recv_sem.at[GATED + block],
                device_id={"ch": group + lax.rem(spot + step, half)},
                device_id_type=MESH,
            ).start()

    def gated_out_done(block):
        return pltpu.make_async_remote_copy(
            src_ref=gated_all.at[pl.ds(0, half - 1), pl.ds(block * R, R)],
            dst_ref=gated_all.at[pl.ds(0, half - 1), pl.ds(block * R, R)],
            send_sem=ch_send_sem.at[GATED + block],
            recv_sem=ch_recv_sem.at[GATED + block],
            device_id={"ch": pair},
            device_id_type=MESH,
        )

    def partial_across(block):
        return pltpu.make_async_remote_copy(
            src_ref=partial_send.at[pl.ds(block * R, R)],
            dst_ref=partial_recv.at[pl.ds(block * R, R)],
            send_sem=ch_send_sem.at[PARTIAL + block],
            recv_sem=ch_recv_sem.at[PARTIAL + block],
            device_id={"ch": pair},
            device_id_type=MESH,
        )

    def opposite(source, target, slot, which, part):
        pltpu.make_async_remote_copy(
            src_ref=source.at[tokens(part)],
            dst_ref=target.at[slot, tokens(part)],
            send_sem=ch_send_sem.at[which + part],
            recv_sem=ch_recv_sem.at[which + part],
            device_id={"ch": group + lax.rem(spot + 2, half)},
            device_id_type=MESH,
        ).start()

    def ring3_done(part, target, which):
        return pltpu.make_async_remote_copy(
            src_ref=target.at[pl.ds(0, 3), tokens(part)],
            dst_ref=target.at[pl.ds(0, 3), tokens(part)],
            send_sem=ch_send_sem.at[which + part],
            recv_sem=ch_recv_sem.at[which + part],
            device_id={"ch": pair},
            device_id_type=MESH,
        )

    def hand_on(target, base, which, part):
        for index, (origin, to) in enumerate(((turn_down, turn_up), (turn_up, turn_down))):
            piece = pl.ds((part * per_part + index) * R, R)
            pltpu.make_async_remote_copy(
                src_ref=target.at[base + origin, piece],
                dst_ref=target.at[base + origin, piece],
                send_sem=ch_send_sem.at[which + part],
                recv_sem=ch_recv_sem.at[which + part],
                device_id={"ch": group + to},
                device_id_type=MESH,
            ).start()

    def hand_on_done(target, which, part):
        return pltpu.make_async_remote_copy(
            src_ref=target.at[0, tokens(part)],
            dst_ref=target.at[0, tokens(part)],
            send_sem=ch_send_sem.at[which + part],
            recv_sem=ch_recv_sem.at[which + part],
            device_id={"ch": pair},
            device_id_type=MESH,
        )

    def across(source, target, which, part):
        return pltpu.make_async_remote_copy(
            src_ref=source.at[tokens(part)],
            dst_ref=target.at[tokens(part)],
            send_sem=ch_send_sem.at[which + part],
            recv_sem=ch_recv_sem.at[which + part],
            device_id={"ch": pair},
            device_id_type=MESH,
        )

    staged = seq_count * each * per_part

    def to_stage(target, which, h):
        for part in range(PARTS):
            target[h, part * staged : (part + 1) * staged, :] = (
                seq_recv[which, h, :, part].astype(F32).reshape(staged, R)
            )

    def from_stage(which, h):
        for part in range(PARTS):
            seq_send[which, h, :, part] = (
                stage[h, part * staged : (part + 1) * staged, :]
                .astype(BF16)
                .reshape(seq_count, each * per_part, R)
            )

    def spectrum(source, h, at):
        signal = jnp.concatenate(
            [source[h, pl.ds(at + two, R, stride=each), :].astype(BF16) for two in range(2)],
            axis=1,
        )
        both = dot(fa[...], jnp.concatenate([signal, signal], axis=0))
        real, imag = both[:R], both[R:]
        turned_re = real * turn[0] - imag * turn[1]
        turned_im = real * turn[1] + imag * turn[0]
        stacked = jnp.concatenate(
            [
                jnp.concatenate([turned_re[:, :R], turned_im[:, :R]], axis=1),
                jnp.concatenate([turned_re[:, R:], turned_im[:, R:]], axis=1),
            ],
            axis=0,
        )
        high, low = split(stacked)
        out = dot(jnp.concatenate([high, low, high], axis=1), fb[...])
        return out[:, :R], out[:, R:]

    def signal_of(real, imag, h, at):
        high, low = split(jnp.concatenate([real, imag], axis=1))
        back = dot(jnp.concatenate([high, low, high], axis=1), ib[...])
        real = jnp.concatenate([back[:R, :R], back[R:, :R]], axis=1)
        imag = jnp.concatenate([back[:R, R:], back[R:, R:]], axis=1)
        turned_re = real * turn[0] + imag * turn[1]
        turned_im = imag * turn[0] - real * turn[1]
        high, low = split(jnp.concatenate([turned_re, turned_im], axis=0))
        out = dot(ia[...], jnp.concatenate([high, low, high], axis=0))
        for two in range(2):
            stage[h, pl.ds(at + two, R, stride=each), :] = out[:, two * R : (two + 1) * R]

    def take_in(which, h, part):
        spread_in[h, part] = seq_recv[which, h, :, part].astype(F32).reshape(staged, R)

    def received(block):
        part, at = block // per_part, block % per_part
        return jnp.concatenate(
            [
                jnp.transpose(
                    jnp.concatenate(
                        [
                            spread_in[
                                h, part, pl.ds(each * at + j, seq_count, stride=each * per_part), :
                            ]
                            for j in range(each)
                        ],
                        axis=0,
                    )
                )
                for h in range(2)
            ],
            axis=1,
        )

    fetches[0].wait()
    for block in range(blocks):
        lay_out(block, taps[rows(block), :])
    for h in range(2):
        for part in range(PARTS):
            laid_out(TAPS, h, part)

    fetches[1].wait()
    fetches[2].wait()
    for block in range(blocks):
        lay_out(block, key[rows(block), :].astype(F32) * value[rows(block), :].astype(F32))
    for h in range(2):
        for part in range(PARTS):
            laid_out(MIXED, h, part)

    pl.semaphore_wait(barrier, seq_count + half - 1)

    ring(out_grad, cotangents, ch_me, COT_OWN, 0)
    across(out_grad, cotangents.at[ch_me], COT_PAIR, 0).start()
    exchange(TAPS, 0, h=0)

    exchange(MIXED, 0, h=0)
    ring(out_grad, cotangents, ch_me, COT_OWN, 1)
    across(out_grad, cotangents.at[ch_me], COT_PAIR, 1).start()
    exchange(TAPS, 1, h=1)
    exchange(MIXED, 1, h=1)

    for fetch in fetches[3:]:
        fetch.wait()

    def cotangent_pair(part):
        across(out_grad, cotangents.at[pair], COT_PAIR, part).wait_recv()
        ring(cotangents.at[pair], cotangents, pair, COT_FAR, part)
        opposite(cotangents.at[pair], cotangents, pair, COT_FAR, part)

    def cotangent_own_on(part):
        ring_done(cotangents, COT_OWN, part).wait_recv()
        hand_on(cotangents, group, COT_OWN_ON, part)

    cotangent_own_on(0)
    cotangent_pair(0)
    cotangent_own_on(1)
    cotangent_pair(1)

    def taps_half(h):
        exchanged(TAPS, h, h=h).wait_recv()
        to_stage(stage_taps, TAPS, h)

        def step(index, carry):
            real, imag = spectrum(stage_taps, h, 2 * index)
            taps_spec[2 * h + index, :, :R] = real
            taps_spec[2 * h + index, :, R:] = imag
            return carry

        lax.fori_loop(0, 2, step, 0, unroll=True)

    def mixed_half(h):
        exchanged(MIXED, h, h=h).wait_recv()
        to_stage(stage, MIXED, h)

        def step(index, carry):
            real, imag = spectrum(stage, h, 2 * index)
            taps_re, taps_im = taps_spec[2 * h + index, :, :R], taps_spec[2 * h + index, :, R:]
            signal_of(
                real * taps_re - imag * taps_im, real * taps_im + imag * taps_re, h, 2 * index
            )
            return carry

        lax.fori_loop(0, 2, step, 0, unroll=True)
        from_stage(CONV, h)

    def cotangent_product(part):
        hand_on_done(cotangents, COT_OWN_ON, part).wait_recv()
        ring3_done(part, cotangents, COT_FAR).wait_recv()
        for block in range(part * per_part, (part + 1) * per_part):
            total = None
            for source in range(ch_count):
                term = lax.dot_general(
                    cotangents[source, rows(block), :],
                    weight[:, source * columns : (source + 1) * columns],
                    (((1,), (1,)), ((), ())),
                    preferred_element_type=F32,
                )
                total = term if total is None else total + term
            grad_gated[rows(block), :] = total
            product = total * query[rows(block), :].astype(F32)
            grad_conv[rows(block), :] = product
            lay_out(block, product)
        for h in range(2):
            laid_out(GRAD, h, part)
        if part == 0:
            exchange(GRAD, 0, part=0)
        else:
            exchange(GRAD, 1, h=0, part=1)
            exchange(GRAD, 2, h=1, part=1)

    taps_half(0)
    mixed_half(0)
    exchange(CONV, 0, h=0)
    cotangent_product(0)
    taps_half(1)
    mixed_half(1)
    exchange(CONV, 1, h=1)

    cotangent_product(1)

    half_rows = columns // 2
    for target in range(2):
        for step in range(1, half):
            to = lax.rem(spot + step, half)
            at = pl.multiple_of((target * half + to) * columns, columns)
            pltpu.make_async_remote_copy(
                src_ref=weight.at[
                    pl.ds(pl.multiple_of(core * half_rows, half_rows), half_rows),
                    pl.ds(at, columns),
                ],
                dst_ref=weight_cols.at[core, spot, target],
                send_sem=ch_send_sem.at[WEIGHT],
                recv_sem=ch_recv_sem.at[WEIGHT],
                device_id={"ch": group + to},
                device_id_type=MESH,
            ).start()
        at = pl.multiple_of((target * half + spot) * columns, columns)
        weight_cols[core, spot, target] = weight[
            pl.ds(pl.multiple_of(core * half_rows, half_rows), half_rows), pl.ds(at, columns)
        ]

    gains = skip[...]
    for part in range(PARTS):
        if part == 0:
            exchanged(CONV, 0, h=0).wait_recv()
            exchanged(CONV, 1, h=1).wait_recv()
        for h in range(2):
            take_in(CONV, h, part)
        for block in range(part * per_part, (part + 1) * per_part):
            mixed = key[rows(block), :].astype(F32) * value[rows(block), :].astype(F32)
            conv = received(block) + gains * mixed
            gated_all[spot, rows(block), :] = (query[rows(block), :].astype(F32) * conv).astype(
                BF16
            )
            query_grad[rows(block), :] = (grad_gated[rows(block), :] * conv).astype(BF16)
            gated_out_to(block)

    pltpu.make_async_remote_copy(
        src_ref=weight_cols.at[0, pl.ds(0, half - 1)],
        dst_ref=weight_cols.at[0, pl.ds(0, half - 1)],
        send_sem=ch_send_sem.at[WEIGHT],
        recv_sem=ch_recv_sem.at[WEIGHT],
        device_id={"ch": pair},
        device_id_type=MESH,
    ).wait()
    to_sibling = pltpu.make_async_remote_copy(
        src_ref=weight_cols.at[core],
        dst_ref=weight_cols.at[core],
        send_sem=ch_send_sem.at[SIBLING],
        recv_sem=ch_recv_sem.at[SIBLING],
        device_id={"seq": sibling},
        device_id_type=MESH,
    )
    to_sibling.start()


    def grad_half(h):
        exchanged(GRAD, 1 + h, h=h, part=1).wait_recv()
        to_stage(stage, GRAD, h)

        def step(index, carry):
            real, imag = spectrum(stage, h, 2 * index)
            taps_re, taps_im = taps_spec[2 * h + index, :, :R], taps_spec[2 * h + index, :, R:]
            signal_of(
                taps_re * real + taps_im * imag, taps_re * imag - taps_im * real, h, 2 * index
            )
            return carry

        lax.fori_loop(0, 2, step, 0, unroll=True)
        from_stage(BACK, h)

    exchanged(GRAD, 0, part=0).wait_recv()
    grad_half(0)
    exchange(BACK, 0, h=0)
    grad_half(1)
    exchange(BACK, 1, h=1)

    to_sibling.wait()

    def project(target, block):
        total = None
        for source in range(half):
            for part in range(2):
                term = dot(
                    gated_all[source, rows(block), part * half_rows : (part + 1) * half_rows],
                    weight_cols[part, source, target],
                )
                total = term if total is None else total + term
        return total

    for block in range(blocks):
        gated_out_done(block).wait_recv()
        partial_send[rows(block), :] = project(1 - side, block).astype(BF16)
        partial_across(block).start()
        grad_gated[rows(block), :] = project(side, block)

    for part in range(PARTS):
        if part == 0:
            exchanged(BACK, 0, h=0).wait_recv()
            exchanged(BACK, 1, h=1).wait_recv()
        for h in range(2):
            take_in(BACK, h, part)
        for block in range(part * per_part, (part + 1) * per_part):
            total = received(block) + gains * grad_conv[rows(block), :]
            key_grad[rows(block), :] = (total * value[rows(block), :].astype(F32)).astype(BF16)
            value_grad[rows(block), :] = (total * key[rows(block), :].astype(F32)).astype(BF16)

    for block in range(blocks):
        partial_across(block).wait_recv()
        mixed_out[rows(block), :] = (
            grad_gated[rows(block), :] + partial_recv[rows(block), :].astype(F32)
        ).astype(BF16)

    for h in range(2):
        exchanged(TAPS, h, h=h).wait_send()
        exchanged(MIXED, h, h=h).wait_send()
        exchanged(GRAD, 1 + h, h=h, part=1).wait_send()
    exchanged(GRAD, 0, part=0).wait_send()
    for which in (CONV, BACK):
        exchanged(which, 0, h=0).wait_send()
        exchanged(which, 1, h=1).wait_send()
    for part in range(PARTS):
        across(out_grad, cotangents.at[ch_me], COT_PAIR, part).wait_send()
        ring_done(cotangents, COT_OWN, part).wait_send()
        hand_on_done(cotangents, COT_OWN_ON, part).wait_send()
        ring3_done(part, cotangents, COT_FAR).wait_send()
    for block in range(blocks):
        gated_out_done(block).wait_send()
        partial_across(block).wait_send()


def hand_out_kernel(count, *refs):
    sources, targets, sem = refs[:count], refs[count : 2 * count], refs[2 * count]
    copies = [
        pltpu.make_async_copy(source, target, sem.at[index])
        for index, (source, target) in enumerate(zip(sources, targets))
    ]
    for copy in copies:
        copy.start()
    for copy in copies:
        copy.wait()


def on_device(query_in, key_in, value_in, filter_taps, skip_gain, out_weight, out_grad):
    seq_count = lax.axis_size("seq")
    ch_count = lax.axis_size("ch")
    row_count, columns = query_in.shape
    blocks = row_count // R
    half = ch_count // 2
    constants = tuple(jnp.asarray(table) for table in tables())
    operands = (
        query_in,
        key_in,
        value_in,
        filter_taps,
        skip_gain.reshape(1, columns),
        out_weight,
        out_grad,
    ) + constants
    operands = tuple(pltpu.with_memory_space_constraint(each, pltpu.HBM) for each in operands)
    in_hbm = pl.BlockSpec(memory_space=pltpu.HBM)
    in_vmem = pl.BlockSpec(memory_space=pltpu.VMEM)
    block_shape = (row_count, columns)
    results = pl.pallas_call(
        functools.partial(layer_kernel, seq_count, ch_count),
        out_shape=[jax.ShapeDtypeStruct(block_shape, BF16)] * 4,
        in_specs=[in_hbm] * len(operands),
        out_specs=[in_vmem] * 4,
        scratch_shapes=[
            pltpu.VMEM(block_shape, BF16),
            pltpu.VMEM(block_shape, BF16),
            pltpu.VMEM(block_shape, BF16),
            pltpu.VMEM(block_shape, F32),
            pltpu.VMEM((1, columns), F32),
            pltpu.VMEM(out_weight.shape, BF16),
        ]
        + [pltpu.VMEM(table.shape, table.dtype) for table in constants]
        + [
            pltpu.VMEM((5, 2, seq_count, PARTS, 8, R), BF16),
            pltpu.VMEM((5, 2, seq_count, PARTS, 8, R), BF16),
            pltpu.VMEM((2, PARTS, 8 * seq_count, R), F32),
            pltpu.VMEM((2, PARTS, 8 * seq_count, R), F32),
            pltpu.VMEM((2, 4 * R, R), F32),
            pltpu.VMEM((2, 4 * R, R), F32),
            pltpu.VMEM((4, 2 * R, 2 * R), F32),
            pltpu.VMEM((ch_count, row_count, columns), BF16),
            pltpu.VMEM((half, row_count, columns), BF16),
            pltpu.VMEM((2, half, 2, columns // 2, columns), BF16),
            pltpu.VMEM(block_shape, BF16),
            pltpu.VMEM(block_shape, BF16),
            pltpu.VMEM(block_shape, F32),
            pltpu.VMEM(block_shape, F32),
            pltpu.SemaphoreType.DMA((15,)),
            pltpu.SemaphoreType.DMA((15,)),
            pltpu.SemaphoreType.DMA((18,)),
            pltpu.SemaphoreType.DMA((18,)),
            pltpu.SemaphoreType.DMA((12,)),
        ],
        compiler_params=pltpu.CompilerParams(
            collective_id=0, has_side_effects=True, vmem_limit_bytes=48 * 1024 * 1024
        ),
        name="layer",
    )(*operands)
    return pl.pallas_call(
        functools.partial(hand_out_kernel, len(results)),
        out_shape=[jax.ShapeDtypeStruct(block_shape, BF16)] * 4,
        in_specs=[in_vmem] * 4,
        out_specs=[in_hbm] * 4,
        scratch_shapes=[pltpu.SemaphoreType.DMA((4,))],
        name="hand_out",
    )(*[pltpu.with_memory_space_constraint(each, pltpu.VMEM) for each in results])


def solution(mesh):
    placed = (
        P("seq", "ch"),
        P("seq", "ch"),
        P("seq", "ch"),
        P("seq", "ch"),
        P("ch"),
        P("ch", None),
        P("seq", "ch"),
    )
    return jax.shard_map(
        on_device,
        mesh=mesh,
        in_specs=placed,
        out_specs=(P("seq", "ch"), P("seq", "ch"), P("seq", "ch"), P("seq", "ch")),
        check_vma=False,
    )
```

```python
import functools
import math

import jax
import jax.numpy as jnp
import numpy as np
from jax import lax
from jax.experimental import pallas as pl
from jax.experimental.pallas import tpu as pltpu
from jax.sharding import PartitionSpec as P

F32 = jnp.float32
BF16 = jnp.bfloat16
MESH = pl.DeviceIdType.MESH

R = 128
L = R * R


def split_table(table):
    high = table.astype(np.float32).astype(jnp.bfloat16)
    low = (table - high.astype(np.float64)).astype(np.float32).astype(jnp.bfloat16)
    return high, low


def tables():
    n = np.arange(R, dtype=np.float64)
    p = n + 0.25
    first = np.exp(-2j * math.pi * np.outer(p, n) / R)
    turn = np.exp(-2j * math.pi * np.outer(p, n) / L)
    second = np.exp(-2j * math.pi * np.outer(n, n) / R)
    place = np.arange(R)
    order = 4 * (place % 64 // 2) + 2 * (place // 64) + place % 2
    first = first[:, order]
    forward_a = np.concatenate([first.real, first.imag], axis=0)
    forward_b = np.block([[second.real, second.imag], [-second.imag, second.real]])
    inverse_b = forward_b.T
    inverse_a = np.concatenate([first.real.T, first.imag.T], axis=1) / L
    fa_high, fa_low = split_table(forward_a)
    fb_high, fb_low = split_table(forward_b)
    ib_high, ib_low = split_table(inverse_b)
    ia_high, ia_low = split_table(inverse_a)
    turns = np.stack([turn.real, turn.imag]).astype(np.float32)
    return (
        np.concatenate([fa_high, fa_low], axis=1),
        np.concatenate([fb_high, fb_high, fb_low], axis=0),
        np.concatenate([ib_high, ib_high, ib_low], axis=0),
        np.concatenate([ia_high, ia_high, ia_low], axis=1),
        np.concatenate([turns, turns], axis=2),
    )


def split(values):
    high = values.astype(BF16)
    low = (values - high.astype(F32)).astype(BF16)
    return high, low


def dot(left, right):
    return jnp.dot(left, right, preferred_element_type=F32)


TAPS, MIXED, CONV, GRAD, BACK = range(5)
COT_PAIR, COT_OWN, COT_OWN_ON, COT_FAR = range(0, 8, 2)
WEIGHT, SIBLING, GATED, PARTIAL = 8, 9, 10, 14
PARTS = 2


def layer_kernel(
    seq_count,
    ch_count,
    query_hbm,
    key_hbm,
    value_hbm,
    taps_hbm,
    skip_hbm,
    weight_hbm,
    out_grad,
    fa_hbm,
    fb_hbm,
    ib_hbm,
    ia_hbm,
    turn_hbm,
    mixed_out,
    query_grad,
    key_grad,
    value_grad,
    query,
    key,
    value,
    taps,
    skip,
    weight,
    fa,
    fb,
    ib,
    ia,
    turn,
    seq_send,
    seq_recv,
    spread_out,
    spread_in,
    stage_taps,
    stage,
    taps_spec,
    cotangents,
    gated_all,
    weight_cols,
    partial_send,
    partial_recv,
    grad_gated,
    grad_conv,
    conv_all,
    seq_send_sem,
    seq_recv_sem,
    ch_send_sem,
    ch_recv_sem,
    local_sem,
):
    seq_me = lax.axis_index("seq")
    ch_me = lax.axis_index("ch")
    row_count, columns = query.shape
    blocks = row_count // R
    half = ch_count // 2
    pair = lax.rem(ch_me + half, ch_count)
    side = ch_me // half
    group = side * half
    spot = lax.rem(ch_me, half)
    core = lax.rem(seq_me, 2)
    sibling = seq_me + 1 - 2 * core
    turn_up = lax.rem(spot + 1, half)
    turn_down = lax.rem(spot + half - 1, half)
    per_part = blocks // PARTS
    part_rows = row_count // PARTS

    fetches = [
        pltpu.make_async_copy(source, target, local_sem.at[index])
        for index, (source, target) in enumerate(
            (
                (taps_hbm, taps),
                (key_hbm, key),
                (value_hbm, value),
                (out_grad, cotangents.at[ch_me]),
                (fa_hbm, fa),
                (turn_hbm, turn),
                (fb_hbm, fb),
                (ib_hbm, ib),
                (ia_hbm, ia),
                (weight_hbm, weight),
                (query_hbm, query),
                (skip_hbm, skip),
            )
        )
    ]
    for fetch in fetches[:3]:
        fetch.start()

    barrier = pltpu.get_barrier_semaphore()

    def greet_seq(step, carry):
        peer = lax.rem(seq_me + step, seq_count)
        pl.semaphore_signal(barrier, inc=1, device_id={"seq": peer}, device_id_type=MESH)
        return carry

    lax.fori_loop(1, seq_count, greet_seq, 0)
    for step in range(1, half):
        peer = group + lax.rem(spot + step, half)
        pl.semaphore_signal(barrier, inc=1, device_id={"ch": peer}, device_id_type=MESH)
    pl.semaphore_signal(barrier, inc=1, device_id={"ch": pair}, device_id_type=MESH)

    for fetch in fetches[3:]:
        fetch.start()

    def rows(block):
        return slice(block * R, (block + 1) * R)

    width = columns // 2
    each = width // seq_count

    def lay_out(block, values):
        part, at = block // per_part, block % per_part
        for h in range(2):
            turned = jnp.transpose(values[:, h * width : (h + 1) * width])
            for j in range(each):
                spread_out[
                    h, part, pl.ds(each * at + j, seq_count, stride=each * per_part), :
                ] = turned[seq_count * j : seq_count * (j + 1)]

    def laid_out(which, h, part):
        seq_send[which, h, :, part] = (
            spread_out[h, part].astype(BF16).reshape(seq_count, each * per_part, R)
        )

    def span_of(h, part):
        halves = pl.ds(0, 2) if h is None else pl.ds(h, 1)
        parts = pl.ds(0, PARTS) if part is None else pl.ds(part, 1)
        return halves, parts

    def exchange(which, sem, h=None, part=None):
        halves, parts = span_of(h, part)

        def step(index, carry):
            peer = lax.rem(seq_me + index, seq_count)
            pltpu.make_async_remote_copy(
                src_ref=seq_send.at[which, halves, peer, parts],
                dst_ref=seq_recv.at[which, halves, seq_me, parts],
                send_sem=seq_send_sem.at[3 * which + sem],
                recv_sem=seq_recv_sem.at[3 * which + sem],
                device_id={"seq": peer},
                device_id_type=MESH,
            ).start()
            return carry

        lax.fori_loop(1, seq_count, step, 0)
        for one_h in (0, 1) if h is None else (h,):
            for one_part in range(PARTS) if part is None else (part,):
                seq_recv[which, one_h, seq_me, one_part] = seq_send[
                    which, one_h, seq_me, one_part
                ]

    def exchanged(which, sem, h=None, part=None):
        halves, parts = span_of(h, part)
        return pltpu.make_async_remote_copy(
            src_ref=seq_send.at[which, halves, pl.ds(0, seq_count - 1), parts],
            dst_ref=seq_recv.at[which, halves, pl.ds(0, seq_count - 1), parts],
            send_sem=seq_send_sem.at[3 * which + sem],
            recv_sem=seq_recv_sem.at[3 * which + sem],
            device_id={"seq": sibling},
            device_id_type=MESH,
        )

    def tokens(part):
        return pl.ds(part * part_rows, part_rows)

    def ring(source, target, slot, which, part):
        for to in (turn_up, turn_down):
            pltpu.make_async_remote_copy(
                src_ref=source.at[tokens(part)],
                dst_ref=target.at[slot, tokens(part)],
                send_sem=ch_send_sem.at[which + part],
                recv_sem=ch_recv_sem.at[which + part],
                device_id={"ch": group + to},
                device_id_type=MESH,
            ).start()

    def ring_done(target, which, part):
        return pltpu.make_async_remote_copy(
            src_ref=target.at[pl.ds(0, 2), tokens(part)],
            dst_ref=target.at[pl.ds(0, 2), tokens(part)],
            send_sem=ch_send_sem.at[which + part],
            recv_sem=ch_recv_sem.at[which + part],
            device_id={"ch": pair},
            device_id_type=MESH,
        )

    def gated_out_to(block):
        for step in (1, half - 1, 2):
            pltpu.make_async_remote_copy(
                src_ref=gated_all.at[spot, pl.ds(block * R, R)],
                dst_ref=gated_all.at[spot, pl.ds(block * R, R)],
                send_sem=ch_send_sem.at[GATED + block],
                recv_sem=ch_recv_sem.at[GATED + block],
                device_id={"ch": group + lax.rem(spot + step, half)},
                device_id_type=MESH,
            ).start()

    def gated_out_done(block):
        return pltpu.make_async_remote_copy(
            src_ref=gated_all.at[pl.ds(0, half - 1), pl.ds(block * R, R)],
            dst_ref=gated_all.at[pl.ds(0, half - 1), pl.ds(block * R, R)],
            send_sem=ch_send_sem.at[GATED + block],
            recv_sem=ch_recv_sem.at[GATED + block],
            device_id={"ch": pair},
            device_id_type=MESH,
        )

    def partial_across(block):
        return pltpu.make_async_remote_copy(
            src_ref=partial_send.at[pl.ds(block * R, R)],
            dst_ref=partial_recv.at[pl.ds(block * R, R)],
            send_sem=ch_send_sem.at[PARTIAL + block],
            recv_sem=ch_recv_sem.at[PARTIAL + block],
            device_id={"ch": pair},
            device_id_type=MESH,
        )

    def opposite(source, target, slot, which, part):
        pltpu.make_async_remote_copy(
            src_ref=source.at[tokens(part)],
            dst_ref=target.at[slot, tokens(part)],
            send_sem=ch_send_sem.at[which + part],
            recv_sem=ch_recv_sem.at[which + part],
            device_id={"ch": group + lax.rem(spot + 2, half)},
            device_id_type=MESH,
        ).start()

    def ring3_done(part, target, which):
        return pltpu.make_async_remote_copy(
            src_ref=target.at[pl.ds(0, 3), tokens(part)],
            dst_ref=target.at[pl.ds(0, 3), tokens(part)],
            send_sem=ch_send_sem.at[which + part],
            recv_sem=ch_recv_sem.at[which + part],
            device_id={"ch": pair},
            device_id_type=MESH,
        )

    def hand_on(target, base, which, part):
        for index, (origin, to) in enumerate(((turn_down, turn_up), (turn_up, turn_down))):
            piece = pl.ds((part * per_part + index) * R, R)
            pltpu.make_async_remote_copy(
                src_ref=target.at[base + origin, piece],
                dst_ref=target.at[base + origin, piece],
                send_sem=ch_send_sem.at[which + part],
                recv_sem=ch_recv_sem.at[which + part],
                device_id={"ch": group + to},
                device_id_type=MESH,
            ).start()

    def hand_on_done(target, which, part):
        return pltpu.make_async_remote_copy(
            src_ref=target.at[0, tokens(part)],
            dst_ref=target.at[0, tokens(part)],
            send_sem=ch_send_sem.at[which + part],
            recv_sem=ch_recv_sem.at[which + part],
            device_id={"ch": pair},
            device_id_type=MESH,
        )

    def across(source, target, which, part):
        return pltpu.make_async_remote_copy(
            src_ref=source.at[tokens(part)],
            dst_ref=target.at[tokens(part)],
            send_sem=ch_send_sem.at[which + part],
            recv_sem=ch_recv_sem.at[which + part],
            device_id={"ch": pair},
            device_id_type=MESH,
        )

    staged = seq_count * each * per_part

    def to_stage(target, which, h):
        for part in range(PARTS):
            target[h, part * staged : (part + 1) * staged, :] = (
                seq_recv[which, h, :, part].astype(F32).reshape(staged, R)
            )

    def from_stage(which, h):
        for part in range(PARTS):
            seq_send[which, h, :, part] = (
                stage[h, part * staged : (part + 1) * staged, :]
                .astype(BF16)
                .reshape(seq_count, each * per_part, R)
            )

    def spectrum(source, h, at):
        signal = jnp.concatenate(
            [source[h, pl.ds(at + two, R, stride=each), :].astype(BF16) for two in range(2)],
            axis=1,
        )
        both = dot(fa[...], jnp.concatenate([signal, signal], axis=0))
        real, imag = both[:R], both[R:]
        turned_re = real * turn[0] - imag * turn[1]
        turned_im = real * turn[1] + imag * turn[0]
        stacked = jnp.concatenate(
            [
                jnp.concatenate([turned_re[:, :R], turned_im[:, :R]], axis=1),
                jnp.concatenate([turned_re[:, R:], turned_im[:, R:]], axis=1),
            ],
            axis=0,
        )
        high, low = split(stacked)
        out = dot(jnp.concatenate([high, low, high], axis=1), fb[...])
        return out[:, :R], out[:, R:]

    def signal_of(real, imag, h, at):
        high, low = split(jnp.concatenate([real, imag], axis=1))
        back = dot(jnp.concatenate([high, low, high], axis=1), ib[...])
        real = jnp.concatenate([back[:R, :R], back[R:, :R]], axis=1)
        imag = jnp.concatenate([back[:R, R:], back[R:, R:]], axis=1)
        turned_re = real * turn[0] + imag * turn[1]
        turned_im = imag * turn[0] - real * turn[1]
        high, low = split(jnp.concatenate([turned_re, turned_im], axis=0))
        out = dot(ia[...], jnp.concatenate([high, low, high], axis=0))
        for two in range(2):
            stage[h, pl.ds(at + two, R, stride=each), :] = out[:, two * R : (two + 1) * R]

    def take_in(which, h, part):
        spread_in[h, part] = seq_recv[which, h, :, part].astype(F32).reshape(staged, R)

    def received(block):
        part, at = block // per_part, block % per_part
        return jnp.concatenate(
            [
                jnp.transpose(
                    jnp.concatenate(
                        [
                            spread_in[
                                h, part, pl.ds(each * at + j, seq_count, stride=each * per_part), :
                            ]
                            for j in range(each)
                        ],
                        axis=0,
                    )
                )
                for h in range(2)
            ],
            axis=1,
        )

    fetches[0].wait()
    for block in range(blocks):
        lay_out(block, taps[rows(block), :])
    for h in range(2):
        for part in range(PARTS):
            laid_out(TAPS, h, part)

    fetches[1].wait()
    fetches[2].wait()
    for block in range(blocks):
        lay_out(block, key[rows(block), :].astype(F32) * value[rows(block), :].astype(F32))
    for h in range(2):
        for part in range(PARTS):
            laid_out(MIXED, h, part)

    pl.semaphore_wait(barrier, seq_count + half - 1)

    ring(out_grad, cotangents, ch_me, COT_OWN, 0)
    across(out_grad, cotangents.at[ch_me], COT_PAIR, 0).start()
    exchange(TAPS, 0, h=0)

    exchange(MIXED, 0, h=0)
    ring(out_grad, cotangents, ch_me, COT_OWN, 1)
    across(out_grad, cotangents.at[ch_me], COT_PAIR, 1).start()
    exchange(TAPS, 1, h=1)
    exchange(MIXED, 1, h=1)

    for fetch in fetches[3:]:
        fetch.wait()

    def cotangent_pair(part):
        across(out_grad, cotangents.at[pair], COT_PAIR, part).wait_recv()
        ring(cotangents.at[pair], cotangents, pair, COT_FAR, part)
        opposite(cotangents.at[pair], cotangents, pair, COT_FAR, part)

    def cotangent_own_on(part):
        ring_done(cotangents, COT_OWN, part).wait_recv()
        hand_on(cotangents, group, COT_OWN_ON, part)

    cotangent_own_on(0)
    cotangent_pair(0)
    cotangent_own_on(1)
    cotangent_pair(1)

    def taps_half(h):
        exchanged(TAPS, h, h=h).wait_recv()
        to_stage(stage_taps, TAPS, h)

        def step(index, carry):
            real, imag = spectrum(stage_taps, h, 2 * index)
            taps_spec[2 * h + index, :, :R] = real
            taps_spec[2 * h + index, :, R:] = imag
            return carry

        lax.fori_loop(0, 2, step, 0, unroll=True)

    def mixed_half(h):
        exchanged(MIXED, h, h=h).wait_recv()
        to_stage(stage, MIXED, h)

        def step(index, carry):
            real, imag = spectrum(stage, h, 2 * index)
            taps_re, taps_im = taps_spec[2 * h + index, :, :R], taps_spec[2 * h + index, :, R:]
            signal_of(
                real * taps_re - imag * taps_im, real * taps_im + imag * taps_re, h, 2 * index
            )
            return carry

        lax.fori_loop(0, 2, step, 0, unroll=True)
        from_stage(CONV, h)

    def cotangent_product(part):
        hand_on_done(cotangents, COT_OWN_ON, part).wait_recv()
        ring3_done(part, cotangents, COT_FAR).wait_recv()
        for block in range(part * per_part, (part + 1) * per_part):
            total = None
            for source in range(ch_count):
                term = lax.dot_general(
                    cotangents[source, rows(block), :],
                    weight[:, source * columns : (source + 1) * columns],
                    (((1,), (1,)), ((), ())),
                    preferred_element_type=F32,
                )
                total = term if total is None else total + term
            grad_gated[rows(block), :] = total
            product = total * query[rows(block), :].astype(F32)
            grad_conv[rows(block), :] = product
            lay_out(block, product)
        for h in range(2):
            laid_out(GRAD, h, part)
        if part == 0:
            exchange(GRAD, 0, part=0)
        else:
            exchange(GRAD, 1, h=0, part=1)
            exchange(GRAD, 2, h=1, part=1)

    taps_half(0)
    mixed_half(0)
    exchange(CONV, 0, h=0)
    cotangent_product(0)
    taps_half(1)
    mixed_half(1)
    exchange(CONV, 1, h=1)

    cotangent_product(1)

    half_rows = columns // 2
    for target in range(2):
        for step in range(1, half):
            to = lax.rem(spot + step, half)
            at = pl.multiple_of((target * half + to) * columns, columns)
            pltpu.make_async_remote_copy(
                src_ref=weight.at[
                    pl.ds(pl.multiple_of(core * half_rows, half_rows), half_rows),
                    pl.ds(at, columns),
                ],
                dst_ref=weight_cols.at[core, spot, target],
                send_sem=ch_send_sem.at[WEIGHT],
                recv_sem=ch_recv_sem.at[WEIGHT],
                device_id={"ch": group + to},
                device_id_type=MESH,
            ).start()
        at = pl.multiple_of((target * half + spot) * columns, columns)
        weight_cols[core, spot, target] = weight[
            pl.ds(pl.multiple_of(core * half_rows, half_rows), half_rows), pl.ds(at, columns)
        ]

    gains = skip[...]
    for part in range(PARTS):
        if part == 0:
            exchanged(CONV, 0, h=0).wait_recv()
            exchanged(CONV, 1, h=1).wait_recv()
        for h in range(2):
            take_in(CONV, h, part)
        for block in range(part * per_part, (part + 1) * per_part):
            mixed = key[rows(block), :].astype(F32) * value[rows(block), :].astype(F32)
            conv = received(block) + gains * mixed
            gated_all[spot, rows(block), :] = (query[rows(block), :].astype(F32) * conv).astype(
                BF16
            )
            conv_all[rows(block), :] = conv
            gated_out_to(block)

    pltpu.make_async_remote_copy(
        src_ref=weight_cols.at[0, pl.ds(0, half - 1)],
        dst_ref=weight_cols.at[0, pl.ds(0, half - 1)],
        send_sem=ch_send_sem.at[WEIGHT],
        recv_sem=ch_recv_sem.at[WEIGHT],
        device_id={"ch": pair},
        device_id_type=MESH,
    ).wait()
    to_sibling = pltpu.make_async_remote_copy(
        src_ref=weight_cols.at[core],
        dst_ref=weight_cols.at[core],
        send_sem=ch_send_sem.at[SIBLING],
        recv_sem=ch_recv_sem.at[SIBLING],
        device_id={"seq": sibling},
        device_id_type=MESH,
    )
    to_sibling.start()
    query_grad[...] = (grad_gated[...] * conv_all[...]).astype(BF16)


    def grad_half(h):
        exchanged(GRAD, 1 + h, h=h, part=1).wait_recv()
        to_stage(stage, GRAD, h)

        def step(index, carry):
            real, imag = spectrum(stage, h, 2 * index)
            taps_re, taps_im = taps_spec[2 * h + index, :, :R], taps_spec[2 * h + index, :, R:]
            signal_of(
                taps_re * real + taps_im * imag, taps_re * imag - taps_im * real, h, 2 * index
            )
            return carry

        lax.fori_loop(0, 2, step, 0, unroll=True)
        from_stage(BACK, h)

    exchanged(GRAD, 0, part=0).wait_recv()
    grad_half(0)
    exchange(BACK, 0, h=0)
    grad_half(1)
    exchange(BACK, 1, h=1)

    to_sibling.wait()

    def project(target, block):
        total = None
        for source in range(half):
            for part in range(2):
                term = dot(
                    gated_all[source, rows(block), part * half_rows : (part + 1) * half_rows],
                    weight_cols[part, source, target],
                )
                total = term if total is None else total + term
        return total

    for block in range(blocks):
        gated_out_done(block).wait_recv()
        partial_send[rows(block), :] = project(1 - side, block).astype(BF16)
        partial_across(block).start()
        grad_gated[rows(block), :] = project(side, block)

    for part in range(PARTS):
        if part == 0:
            exchanged(BACK, 0, h=0).wait_recv()
            exchanged(BACK, 1, h=1).wait_recv()
        for h in range(2):
            take_in(BACK, h, part)
        for block in range(part * per_part, (part + 1) * per_part):
            total = received(block) + gains * grad_conv[rows(block), :]
            key_grad[rows(block), :] = (total * value[rows(block), :].astype(F32)).astype(BF16)
            value_grad[rows(block), :] = (total * key[rows(block), :].astype(F32)).astype(BF16)

    for block in range(blocks):
        partial_across(block).wait_recv()
        mixed_out[rows(block), :] = (
            grad_gated[rows(block), :] + partial_recv[rows(block), :].astype(F32)
        ).astype(BF16)

    for h in range(2):
        exchanged(TAPS, h, h=h).wait_send()
        exchanged(MIXED, h, h=h).wait_send()
        exchanged(GRAD, 1 + h, h=h, part=1).wait_send()
    exchanged(GRAD, 0, part=0).wait_send()
    for which in (CONV, BACK):
        exchanged(which, 0, h=0).wait_send()
        exchanged(which, 1, h=1).wait_send()
    for part in range(PARTS):
        across(out_grad, cotangents.at[ch_me], COT_PAIR, part).wait_send()
        ring_done(cotangents, COT_OWN, part).wait_send()
        hand_on_done(cotangents, COT_OWN_ON, part).wait_send()
        ring3_done(part, cotangents, COT_FAR).wait_send()
    for block in range(blocks):
        gated_out_done(block).wait_send()
        partial_across(block).wait_send()


def hand_out_kernel(count, *refs):
    sources, targets, sem = refs[:count], refs[count : 2 * count], refs[2 * count]
    copies = [
        pltpu.make_async_copy(source, target, sem.at[index])
        for index, (source, target) in enumerate(zip(sources, targets))
    ]
    for copy in copies:
        copy.start()
    for copy in copies:
        copy.wait()


def on_device(query_in, key_in, value_in, filter_taps, skip_gain, out_weight, out_grad):
    seq_count = lax.axis_size("seq")
    ch_count = lax.axis_size("ch")
    row_count, columns = query_in.shape
    blocks = row_count // R
    half = ch_count // 2
    constants = tuple(jnp.asarray(table) for table in tables())
    operands = (
        query_in,
        key_in,
        value_in,
        filter_taps,
        skip_gain.reshape(1, columns),
        out_weight,
        out_grad,
    ) + constants
    operands = tuple(pltpu.with_memory_space_constraint(each, pltpu.HBM) for each in operands)
    in_hbm = pl.BlockSpec(memory_space=pltpu.HBM)
    in_vmem = pl.BlockSpec(memory_space=pltpu.VMEM)
    block_shape = (row_count, columns)
    results = pl.pallas_call(
        functools.partial(layer_kernel, seq_count, ch_count),
        out_shape=[jax.ShapeDtypeStruct(block_shape, BF16)] * 4,
        in_specs=[in_hbm] * len(operands),
        out_specs=[in_vmem] * 4,
        scratch_shapes=[
            pltpu.VMEM(block_shape, BF16),
            pltpu.VMEM(block_shape, BF16),
            pltpu.VMEM(block_shape, BF16),
            pltpu.VMEM(block_shape, F32),
            pltpu.VMEM((1, columns), F32),
            pltpu.VMEM(out_weight.shape, BF16),
        ]
        + [pltpu.VMEM(table.shape, table.dtype) for table in constants]
        + [
            pltpu.VMEM((5, 2, seq_count, PARTS, 8, R), BF16),
            pltpu.VMEM((5, 2, seq_count, PARTS, 8, R), BF16),
            pltpu.VMEM((2, PARTS, 8 * seq_count, R), F32),
            pltpu.VMEM((2, PARTS, 8 * seq_count, R), F32),
            pltpu.VMEM((2, 4 * R, R), F32),
            pltpu.VMEM((2, 4 * R, R), F32),
            pltpu.VMEM((4, 2 * R, 2 * R), F32),
            pltpu.VMEM((ch_count, row_count, columns), BF16),
            pltpu.VMEM((half, row_count, columns), BF16),
            pltpu.VMEM((2, half, 2, columns // 2, columns), BF16),
            pltpu.VMEM(block_shape, BF16),
            pltpu.VMEM(block_shape, BF16),
            pltpu.VMEM(block_shape, F32),
            pltpu.VMEM(block_shape, F32),
            pltpu.VMEM(block_shape, F32),
            pltpu.SemaphoreType.DMA((15,)),
            pltpu.SemaphoreType.DMA((15,)),
            pltpu.SemaphoreType.DMA((18,)),
            pltpu.SemaphoreType.DMA((18,)),
            pltpu.SemaphoreType.DMA((12,)),
        ],
        compiler_params=pltpu.CompilerParams(
            collective_id=0, has_side_effects=True, vmem_limit_bytes=48 * 1024 * 1024
        ),
        name="layer",
    )(*operands)
    return pl.pallas_call(
        functools.partial(hand_out_kernel, len(results)),
        out_shape=[jax.ShapeDtypeStruct(block_shape, BF16)] * 4,
        in_specs=[in_vmem] * 4,
        out_specs=[in_hbm] * 4,
        scratch_shapes=[pltpu.SemaphoreType.DMA((4,))],
        name="hand_out",
    )(*[pltpu.with_memory_space_constraint(each, pltpu.VMEM) for each in results])


def solution(mesh):
    placed = (
        P("seq", "ch"),
        P("seq", "ch"),
        P("seq", "ch"),
        P("seq", "ch"),
        P("ch"),
        P("ch", None),
        P("seq", "ch"),
    )
    return jax.shard_map(
        on_device,
        mesh=mesh,
        in_specs=placed,
        out_specs=(P("seq", "ch"), P("seq", "ch"), P("seq", "ch"), P("seq", "ch")),
        check_vma=False,
    )
```
